1024 devices in a mesh: dp: 4 (over x_lo, core), context: 32 (over z), tensor: 8 (over x_hi, y).
Axes of the slice: x: 4 (x_hi: 2, x_lo: 2; x = x_hi * 2 + x_lo), y: 4, z: 32, core: 2. Of those that a mesh axis runs over, the one named last changes fastest.
Arguments:
- normed: bfloat16 [4, 12288, 8192], P('dp', 'context', 'tensor'), may hold values from -8 to 8
- frozen_query_base: bfloat16 [4, 12288, 8192], P('dp', 'context', 'tensor'), may hold values from -66 to 66
- frozen_key_base: bfloat16 [4, 12288, 1024], P('dp', 'context', 'tensor'), may hold values from -3 to 3
- frozen_value_base: bfloat16 [4, 12288, 1024], P('dp', 'context', 'tensor'), may hold values from -4 to 4
- adapter_down_weight: bfloat16 [8192, 48], P('tensor'), may hold values from -0.0625 to 0.0625
- query_up_weight: bfloat16 [16, 8192], P(None, 'tensor'), may hold values from -0.29882812 to 0.29882812
- key_value_up_weight: bfloat16 [2, 16, 1024], P(None, None, 'tensor'), may hold values from -0.29882812 to 0.29882812
- output_gradient: bfloat16 [4, 12288, 8192], P('dp', 'context', 'tensor'), may hold values from -0.02734375 to 0.02734375
Outputs:
- attended: bfloat16 [4, 12288, 8192], P('dp', 'context', 'tensor')
- grad_a: float32 [8192, 48], P('tensor')
- query_up_gradient: float32 [16, 8192], P(None, 'tensor')
- grad_bkv: float32 [2, 16, 1024], P(None, None, 'tensor')
The draws below stay inside these ranges and needn't reach their ends.
All inputs are finite; a program needn't handle non-finite values.
Results may differ from the reference program's by a relative error of at most 0.012.
Values may be sent and summed in bfloat16 or wider, within the bound.
A program may use at most 32 MiB of HBM per device.

```python
import jax
import jax.numpy as jnp
from jax import lax

MODEL_WIDTH = 8192
QUERY_HEAD_COUNT = 64
KEY_VALUE_HEADS = 8
HEAD_SIZE = 128
ADAPTER_DEPTH = 16
TOK_DEV = 384
LENGTH = 12288
SEQS = 4


def drawn(key):
    key_x = jax.random.fold_in(key, 101)
    key_k = jax.random.fold_in(key, 102)
    key_q = jax.random.fold_in(key, 103)
    hidden_x = jnp.clip(jax.random.normal(key_x, (SEQS, LENGTH, MODEL_WIDTH), jnp.float32), -4.0, 4.0)
    key_vals = jnp.clip(jax.random.normal(key_k, (SEQS, LENGTH, KEY_VALUE_HEADS, HEAD_SIZE), jnp.float32), -3.0, 3.0)
    query_vals = jnp.clip(jax.random.normal(key_q, (SEQS, LENGTH, QUERY_HEAD_COUNT, HEAD_SIZE), jnp.float32), -3.0, 3.0)
    return (hidden_x, query_vals.reshape(SEQS, LENGTH, QUERY_HEAD_COUNT * HEAD_SIZE), key_vals.reshape(SEQS, LENGTH, KEY_VALUE_HEADS * HEAD_SIZE))


def draw_normed(key, part):
    return drawn(key)[0].astype(jnp.bfloat16)


def draw_frozen_query_base(key, part):
    return drawn(key)[1].astype(jnp.bfloat16)


def draw_frozen_key_base(key, part):
    return drawn(key)[2].astype(jnp.bfloat16)


def levels(key, dims, cuts, smallest, high):
    level = 1.0
    for position, blocks in cuts:
        steps = jax.random.uniform(jax.random.fold_in(jax.random.fold_in(key, 6), position), (blocks,), jnp.float32, smallest / len(cuts), high / len(cuts))
        level = level * jnp.repeat(jnp.exp(steps), dims[position] // blocks).reshape((-1,) + (1,) * (len(dims) - 1 - position))
    return level


def noise(own_key, extent, spread, reach, split=(), dtype=jnp.bfloat16):
    drawn = jax.random.normal(own_key, extent, jnp.float32) * spread
    if len(split) > 0:
        drawn = levels(own_key, extent, split, -0.22, 0.18) * drawn
    return jnp.clip(drawn, min=-reach, max=reach).astype(dtype)


def setup_inputs(seed: int = 0) -> dict:
    arg_keys = jax.random.split(jax.random.key(seed), 9)
    normed = draw_normed(jax.random.fold_in(arg_keys[8], 71), 0)
    frozen_query_base = draw_frozen_query_base(jax.random.fold_in(arg_keys[8], 71), 0)
    frozen_key_base = draw_frozen_key_base(jax.random.fold_in(arg_keys[8], 71), 0)
    frozen_value_base = noise(arg_keys[3], (SEQS, LENGTH, KEY_VALUE_HEADS * HEAD_SIZE), 1.0, 4.0, ((0, 4), (1, 32), (2, 8)))
    adapter_down_weight = noise(arg_keys[4], (MODEL_WIDTH, 3 * ADAPTER_DEPTH), MODEL_WIDTH ** -0.5, 0.0625, ((0, 8),))
    query_up_weight = noise(arg_keys[5], (ADAPTER_DEPTH, QUERY_HEAD_COUNT * HEAD_SIZE), 0.05, 0.29882812, ((1, 8),))
    key_value_up_weight = noise(arg_keys[6], (2, ADAPTER_DEPTH, KEY_VALUE_HEADS * HEAD_SIZE), 0.05, 0.29882812, ((2, 8),))
    output_gradient = noise(arg_keys[7], (SEQS, LENGTH, QUERY_HEAD_COUNT * HEAD_SIZE), (SEQS * LENGTH) ** -0.5, 0.02734375, ((0, 4), (1, 32), (2, 8)))
    return {"normed": normed, "frozen_query_base": frozen_query_base, "frozen_key_base": frozen_key_base, "frozen_value_base": frozen_value_base, "adapter_down_weight": adapter_down_weight, "query_up_weight": query_up_weight, "key_value_up_weight": key_value_up_weight, "output_gradient": output_gradient}


adapter_scale = 2.0


def attend(query_rows, key_heads, value_heads, grads, allowed):
    scale = HEAD_SIZE ** -0.5
    high = lax.Precision.HIGHEST
    query_full = query_rows.astype(jnp.float32)
    key_full = key_heads.astype(jnp.float32)
    value_full = value_heads.astype(jnp.float32)
    grad_full = grads.astype(jnp.float32)
    scores = jnp.einsum("tgrd,ugd->grtu", query_full, key_full, precision=high) * scale
    masked = jnp.where(allowed, scores, -jnp.inf)
    highest = jnp.max(masked, axis=-1, keepdims=True)
    weights = jnp.exp(masked - highest)
    probs = weights / jnp.sum(weights, axis=-1, keepdims=True)
    probs_low = probs.astype(jnp.bfloat16).astype(jnp.float32)
    output = jnp.einsum("grtu,ugd->tgrd", probs_low, value_full, precision=high)
    prob_grad = jnp.einsum("tgrd,ugd->grtu", grad_full, value_full, precision=high)
    row_dot = jnp.sum(probs * prob_grad, axis=-1, keepdims=True)
    score_grad = (probs * (prob_grad - row_dot) * scale).astype(jnp.bfloat16).astype(jnp.float32)
    query_gradient = jnp.einsum("grtu,ugd->tgrd", score_grad, key_full, precision=high)
    key_gradient = jnp.einsum("grtu,tgrd->ugd", score_grad, query_full, precision=high)
    value_gradient = jnp.einsum("grtu,tgrd->ugd", probs_low, grad_full, precision=high)
    return output, query_gradient, key_gradient, value_gradient


def grouped(query_rows, key_heads, value_heads, grads):
    blocks = query_rows.shape[0] // TOK_DEV
    row_ids = lax.broadcasted_iota(jnp.int32, (TOK_DEV, TOK_DEV), 0)
    col_ids = lax.broadcasted_iota(jnp.int32, (TOK_DEV, TOK_DEV), 1)
    causal = col_ids <= row_ids

    def split_rows(array):
        return array.reshape((blocks, TOK_DEV) + array.shape[1:])

    def one_group(pieces):
        return attend(pieces[0], pieces[1], pieces[2], pieces[3], causal)

    results = lax.map(one_group, (split_rows(query_rows), split_rows(key_heads), split_rows(value_heads), split_rows(grads)))
    return tuple(item.reshape((blocks * TOK_DEV,) + item.shape[2:]) for item in results)


def reference(normed, frozen_query_base, frozen_key_base, frozen_value_base, adapter_down_weight, query_up_weight, key_value_up_weight, output_gradient):
    row_total = SEQS * LENGTH
    flattened = normed.reshape(row_total, MODEL_WIDTH)
    reduced_projection = jnp.dot(flattened, adapter_down_weight, preferred_element_type=jnp.float32).astype(jnp.bfloat16)
    query_rows = (frozen_query_base.reshape(row_total, QUERY_HEAD_COUNT * HEAD_SIZE).astype(jnp.float32) + adapter_scale * jnp.dot(reduced_projection[:, :ADAPTER_DEPTH], query_up_weight, preferred_element_type=jnp.float32)).astype(jnp.bfloat16)
    key_row_block = (frozen_key_base.reshape(row_total, KEY_VALUE_HEADS * HEAD_SIZE).astype(jnp.float32) + adapter_scale * jnp.dot(reduced_projection[:, ADAPTER_DEPTH:2 * ADAPTER_DEPTH], key_value_up_weight[0], preferred_element_type=jnp.float32)).astype(jnp.bfloat16)
    value_row_block = (frozen_value_base.reshape(row_total, KEY_VALUE_HEADS * HEAD_SIZE).astype(jnp.float32) + adapter_scale * jnp.dot(reduced_projection[:, 2 * ADAPTER_DEPTH:], key_value_up_weight[1], preferred_element_type=jnp.float32)).astype(jnp.bfloat16)
    per_group = QUERY_HEAD_COUNT // KEY_VALUE_HEADS
    half_heads = per_group // 2
    offset = TOK_DEV // 2
    query_heads = query_rows.reshape(SEQS, LENGTH, KEY_VALUE_HEADS, per_group, HEAD_SIZE)
    grad_heads = output_gradient.reshape(SEQS, LENGTH, KEY_VALUE_HEADS, per_group, HEAD_SIZE)
    key_heads = key_row_block.reshape(SEQS, LENGTH, KEY_VALUE_HEADS, HEAD_SIZE)
    value_heads = value_row_block.reshape(SEQS, LENGTH, KEY_VALUE_HEADS, HEAD_SIZE)

    def rolled(array):
        return jnp.roll(array, -offset, axis=0)

    def unrolled(array):
        return jnp.roll(array, offset, axis=0)

    outputs, query_grads, key_grads, value_grads = [], [], [], []
    for which in range(SEQS):
        straight = grouped(query_heads[which, :, :, :half_heads], key_heads[which], value_heads[which], grad_heads[which, :, :, :half_heads])
        moved = grouped(rolled(query_heads[which, :, :, half_heads:]), rolled(key_heads[which]), rolled(value_heads[which]), rolled(grad_heads[which, :, :, half_heads:]))
        outputs.append(jnp.concatenate([straight[0], unrolled(moved[0])], axis=2))
        query_grads.append(jnp.concatenate([straight[1], unrolled(moved[1])], axis=2))
        key_grads.append(straight[2] + unrolled(moved[2]))
        value_grads.append(straight[3] + unrolled(moved[3]))
    attended = jnp.stack(outputs).reshape(SEQS, LENGTH, QUERY_HEAD_COUNT * HEAD_SIZE).astype(jnp.bfloat16)
    query_gradient = jnp.stack(query_grads).reshape(row_total, QUERY_HEAD_COUNT * HEAD_SIZE).astype(jnp.bfloat16)
    key_gradient = jnp.stack(key_grads).reshape(row_total, KEY_VALUE_HEADS * HEAD_SIZE).astype(jnp.bfloat16)
    value_gradient = jnp.stack(value_grads).reshape(row_total, KEY_VALUE_HEADS * HEAD_SIZE).astype(jnp.bfloat16)
    spanning_axis = (((0,), (0,)), ((), ()))
    query_up_gradient = adapter_scale * lax.dot_general(reduced_projection[:, :ADAPTER_DEPTH], query_gradient, spanning_axis, preferred_element_type=jnp.float32)
    key_up_gradient = adapter_scale * lax.dot_general(reduced_projection[:, ADAPTER_DEPTH:2 * ADAPTER_DEPTH], key_gradient, spanning_axis, preferred_element_type=jnp.float32)
    value_up_gradient = adapter_scale * lax.dot_general(reduced_projection[:, 2 * ADAPTER_DEPTH:], value_gradient, spanning_axis, preferred_element_type=jnp.float32)
    inner_product = (((1,), (1,)), ((), ()))
    reduced_projection_gradient = (adapter_scale * jnp.concatenate([
        lax.dot_general(query_gradient, query_up_weight, inner_product, preferred_element_type=jnp.float32),
        lax.dot_general(key_gradient, key_value_up_weight[0], inner_product, preferred_element_type=jnp.float32),
        lax.dot_general(value_gradient, key_value_up_weight[1], inner_product, preferred_element_type=jnp.float32)], axis=1)).astype(jnp.bfloat16)
    grad_a = lax.dot_general(flattened, reduced_projection_gradient, spanning_axis, preferred_element_type=jnp.float32)
    return attended, grad_a, query_up_gradient, jnp.stack([key_up_gradient, value_up_gradient])
```

```python
import functools

import jax
import jax.numpy as jnp
from jax import lax
from jax.experimental import pallas as pl
from jax.experimental.pallas import tpu as pltpu
from jax.sharding import Mesh
from jax.sharding import PartitionSpec as P

QUERY_HEAD_COUNT = 64
KEY_VALUE_HEADS = 8
HEAD_SIZE = 128
TENSOR = ("tensor_0", "tensor_1")
DP_CONTEXT = ("dp_0", "dp_1", "context")
DP = ("dp_0", "dp_1")


adapter_scale = 2.0


def cut_along(shard, dim, count):
    dims = shard.shape
    tiles = shard.reshape(*dims[:dim], count, dims[dim] // count, *dims[dim + 1 :])
    return jnp.moveaxis(tiles, dim, 0)


def sent_and_summed(shard, axis, dim):
    count = lax.axis_size(axis)
    tiles = lax.all_to_all(cut_along(shard, dim, count), axis, 0, 0, tiled=True)
    return jnp.sum(tiles, axis=0)


def joined_along(tiles, dim):
    tiles = jnp.moveaxis(tiles, 0, dim)
    dims = tiles.shape
    return tiles.reshape(*dims[:dim], dims[dim] * dims[dim + 1], *dims[dim + 2 :])


def gather_in_order(shard, axes, order):
    tiles = shard
    for k in order:
        tiles = lax.all_gather(tiles, axes[k])
    done = order[::-1]
    back = [done.index(k) for k in range(len(axes))]
    tiles = tiles.transpose(*back, *range(len(axes), tiles.ndim))
    return tiles.reshape(-1, *shard.shape)


def gathered_by_axis(shard, axes, order, dim):
    return joined_along(gather_in_order(shard, axes, order), dim)


def shifted(value, axis, steps):
    count = lax.axis_size(axis)
    pairs = [(source, (source + steps) % count) for source in range(count)]
    return lax.ppermute(value, axis, pairs)


def attend_single(query_rows, key_heads, value_heads, grads, allowed):
    scale = HEAD_SIZE ** (-0.5)
    scores = (
        jnp.einsum("tgd,ugd->gtu", query_rows, key_heads, preferred_element_type=jnp.float32)
        * scale
    )
    masked = jnp.where(allowed, scores, -jnp.inf)
    highest = jnp.max(masked, axis=-1, keepdims=True)
    weights = jnp.exp(masked - highest)
    probs = weights / jnp.sum(weights, axis=-1, keepdims=True)
    probs_low = probs.astype(jnp.bfloat16)
    output = jnp.einsum("gtu,ugd->tgd", probs_low, value_heads, preferred_element_type=jnp.float32)
    prob_grad = jnp.einsum("tgd,ugd->gtu", grads, value_heads, preferred_element_type=jnp.float32)
    row_dot = jnp.sum(probs * prob_grad, axis=-1, keepdims=True)
    score_grad = (probs * (prob_grad - row_dot) * scale).astype(jnp.bfloat16)
    query_gradient = jnp.einsum(
        "gtu,ugd->tgd", score_grad, key_heads, preferred_element_type=jnp.float32
    )
    key_gradient = jnp.einsum(
        "gtu,tgd->ugd", score_grad, query_rows, preferred_element_type=jnp.float32
    )
    value_gradient = jnp.einsum(
        "gtu,tgd->ugd", probs_low, grads, preferred_element_type=jnp.float32
    )
    return (output, query_gradient, key_gradient, value_gradient)


def attend(query_rows, key_heads, value_heads, grads, allowed):

    def one_head(pieces):
        return attend_single(pieces[0], key_heads, value_heads, pieces[1], allowed)

    results = lax.map(one_head, (jnp.moveaxis(query_rows, 2, 0), jnp.moveaxis(grads, 2, 0)))
    output = jnp.moveaxis(results[0], 0, 2)
    query_gradient = jnp.moveaxis(results[1], 0, 2)
    key_gradient = jnp.sum(results[2], axis=0)
    value_gradient = jnp.sum(results[3], axis=0)
    return (output, query_gradient, key_gradient, value_gradient)


def head_count_total(partial_sum):
    share = sent_and_summed(partial_sum, TENSOR, 0)
    return gathered_by_axis(share.astype(jnp.bfloat16), TENSOR, (0, 1), 0)


MESH_ID = pl.DeviceIdType.MESH
F32 = jnp.float32
BF16 = jnp.bfloat16
STEPS = (2, 1, -1, 0)
FAR = (4, 3, 5, 2, 6, 1, 7)


class Place:
    def __init__(self):
        self.x = lax.axis_index("dp_0")
        self.core = lax.axis_index("dp_1")
        self.z = lax.axis_index("context")
        self.half = lax.axis_index("tensor_0")
        self.y = lax.axis_index("tensor_1")
        self.depth = lax.axis_size("context")

    def near(self, a, b, step):
        z = lax.rem(self.z + step + self.depth, self.depth)
        return {
            "dp_0": lax.rem(self.x + a, 2),
            "dp_1": lax.rem(self.core + b, 2),
            "context": z,
        }

    def along(self, step):
        return {"context": lax.rem(self.z + step + self.depth, self.depth)}

    def chunk(self, a, b, step):
        x = lax.rem(self.x + a, 2)
        core = lax.rem(self.core + b, 2)
        return (x * 2 + core) * 4 + lax.rem(self.z + step + 4, 4)


def near_partners():
    for step in STEPS:
        for a in (1, 0):
            for b in (1, 0):
                if a or b or step:
                    yield a, b, step, (a * 2 + b) * 4 + STEPS.index(step)


def remote(src, dst, send_sem, recv_sem, device):
    return pltpu.make_async_remote_copy(
        src_ref=src,
        dst_ref=dst,
        send_sem=send_sem,
        recv_sem=recv_sem,
        device_id=device,
        device_id_type=MESH_ID,
    )


class TensorSum:
    def __init__(self, place, xs, xr, ys, yr, send, recv):
        self.xs, self.xr, self.ys, self.yr = xs, xr, ys, yr
        half = lax.rem(place.half + 1, 2)
        self.first = remote(xs, xr, send.at[0], recv.at[0], {"tensor_0": half})
        self.second = [
            remote(
                ys,
                yr.at[k - 1],
                send.at[k],
                recv.at[k],
                {"tensor_1": lax.rem(place.y + k, 4)},
            )
            for k in (2, 1, 3)
        ]

    def start(self, part):
        self.part = part
        self.xs[...] = part.astype(BF16)
        self.first.start()

    def middle(self):
        self.first.wait()
        self.total = self.part + self.xr[...].astype(F32)
        self.ys[...] = self.total.astype(BF16)
        for copy in self.second:
            copy.start()

    def end(self):
        for copy in self.second:
            copy.wait()
        total = self.total
        for k in range(3):
            total = total + self.yr[k].astype(F32)
        return total


class TokenSum:
    def __init__(self, place, mine, got, spread, full, send, recv):
        self.place = place
        self.mine, self.got, self.spread, self.full = mine, got, spread, full
        own = place.chunk(0, 0, 0)
        self.own = own
        self.group = place.z // 4
        groups = place.depth // 4
        self.first, self.third = [], []
        for a, b, step, slot in near_partners():
            device = place.near(a, b, step)
            self.first.append(
                (
                    slot,
                    remote(
                        mine.at[place.chunk(a, b, step)],
                        got.at[slot],
                        send.at[slot],
                        recv.at[slot],
                        device,
                    ),
                )
            )
            self.third.append(
                remote(
                    full.at[own], full.at[own], send.at[24 + slot], recv.at[24 + slot], device
                )
            )
        self.second = [
            remote(
                spread.at[self.group],
                spread.at[self.group],
                send.at[16 + k],
                recv.at[16 + k],
                place.along(4 * k),
            )
            for k in FAR
        ]
        self.groups = groups

    def start(self):
        for _, copy in self.first:
            copy.start()

    def middle(self):
        total = self.mine[self.own].astype(F32)
        for slot, copy in self.first:
            copy.wait_recv()
            total = total + self.got[slot].astype(F32)
        self.spread[self.group] = total.astype(BF16)
        for copy in self.second:
            copy.start()

    def late(self):
        for copy in self.second:
            copy.wait_recv()
        total = self.spread[0].astype(F32)
        for k in range(1, 8):
            total = total + self.spread[k].astype(F32)
        self.full[self.own] = total.astype(BF16)
        for copy in self.third:
            copy.start()

    def end(self):
        for copy in self.third:
            copy.wait_recv()

    def drain(self):
        for _, copy in self.first:
            copy.wait_send()
        for copy in self.second:
            copy.wait_send()
        for copy in self.third:
            copy.wait_send()


def greet(place):
    barrier = pltpu.get_barrier_semaphore()
    partners = []
    for step in (2, -2, 1, -1, 0):
        for a in (1, 0):
            for b in (1, 0):
                if a or b or step:
                    partners.append(place.near(a, b, step))
    for k in FAR:
        partners.append(place.along(4 * k))
    partners.append({"tensor_0": lax.rem(place.half + 1, 2)})
    for k in (2, 1, 3):
        partners.append({"tensor_1": lax.rem(place.y + k, 4)})
    for device in partners:
        pl.semaphore_signal(barrier, inc=1, device_id=device, device_id_type=MESH_ID)
    pl.semaphore_wait(barrier, len(partners))


def tail_kernel(
    part_ref,
    normed_ref,
    up_ref,
    pair_ref,
    down_out,
    up_out,
    pair_out,
    xs,
    xr,
    ys,
    yr,
    tsend,
    trecv,
    e_mine,
    e_got,
    e_spread,
    e_full,
    esend,
    erecv,
    g_mine,
    g_got,
    g_spread,
    g_full,
    gsend,
    grecv,
):
    place = Place()
    greet(place)
    early = TokenSum(place, e_mine, e_got, e_spread, e_full, esend, erecv)
    late = TokenSum(place, g_mine, g_got, g_spread, g_full, gsend, grecv)
    ranks = TensorSum(place, xs, xr, ys, yr, tsend, trecv)
    ranks.start(part_ref[...])
    zeros = jnp.zeros((8, 128), F32)
    for c in range(16):
        top = up_ref[8 * (c % 2) : 8 * (c % 2) + 8, 128 * (c // 2) : 128 * (c // 2) + 128]
        low = pair_ref[8 * c : 8 * c + 8, :] if c < 4 else zeros
        e_mine[c] = jnp.concatenate([top, low], axis=0).astype(BF16)
    early.start()
    ranks.middle()
    early.middle()
    rank_grad = (adapter_scale * ranks.end()).astype(BF16)
    for j in range(8):
        columns = slice(128 * j, 128 * j + 128)
        down = jnp.dot(rank_grad, normed_ref[:, columns], preferred_element_type=F32)
        g_mine[2 * j] = down[:24].astype(BF16)
        g_mine[2 * j + 1] = down[24:].astype(BF16)
    late.start()
    late.middle()
    early.late()
    early.end()
    for c in range(16):
        value = e_full[c].astype(F32)
        up_out[8 * (c % 2) : 8 * (c % 2) + 8, 128 * (c // 2) : 128 * (c // 2) + 128] = value[:8]
        if c < 4:
            pair_out[8 * c : 8 * c + 8, :] = value[8:]
    late.late()
    late.end()
    for c in range(16):
        down_out[24 * (c % 2) : 24 * (c % 2) + 24, 128 * (c // 2) : 128 * (c // 2) + 128] = g_full[
            c
        ].astype(F32)
    early.drain()
    late.drain()


def token_sum_scratch(rows):
    return [
        pltpu.VMEM((16, rows, 128), BF16),
        pltpu.VMEM((16, rows, 128), BF16),
        pltpu.VMEM((8, rows, 128), BF16),
        pltpu.VMEM((16, rows, 128), BF16),
        pltpu.SemaphoreType.DMA((40,)),
        pltpu.SemaphoreType.DMA((40,)),
    ]


def tail(part, normed, up, pair):
    vmem = pl.BlockSpec(memory_space=pltpu.VMEM)
    ranks, tokens = part.shape
    return pl.pallas_call(
        tail_kernel,
        out_shape=(
            jax.ShapeDtypeStruct((ranks, normed.shape[1]), F32),
            jax.ShapeDtypeStruct(up.shape, F32),
            jax.ShapeDtypeStruct(pair.shape, F32),
        ),
        in_specs=[vmem] * 4,
        out_specs=(vmem,) * 3,
        scratch_shapes=[
            pltpu.VMEM((ranks, tokens), BF16),
            pltpu.VMEM((ranks, tokens), BF16),
            pltpu.VMEM((ranks, tokens), BF16),
            pltpu.VMEM((3, ranks, tokens), BF16),
            pltpu.SemaphoreType.DMA((4,)),
            pltpu.SemaphoreType.DMA((4,)),
        ]
        + token_sum_scratch(16)
        + token_sum_scratch(24),
        compiler_params=pltpu.CompilerParams(collective_id=0, has_side_effects=True),
    )(part, normed, up, pair)


def on_device(
    normed,
    frozen_query_base,
    frozen_key_base,
    frozen_value_base,
    adapter_down_weight,
    query_up_weight,
    key_value_up_weight,
    output_gradient,
):
    token_count = normed[0]
    tok_count = token_count.shape[0]
    half_rows = tok_count // 2
    adapter_depth = query_up_weight.shape[0]
    per_group = QUERY_HEAD_COUNT // KEY_VALUE_HEADS
    half_heads = per_group // 2
    kv_count = frozen_key_base.shape[2] // HEAD_SIZE
    reduced_projection = head_count_total(
        jnp.dot(token_count, adapter_down_weight, preferred_element_type=jnp.float32)
    )
    query_rows = (
        frozen_query_base[0].astype(jnp.float32)
        + adapter_scale
        * jnp.dot(
            reduced_projection[:, :adapter_depth],
            query_up_weight,
            preferred_element_type=jnp.float32,
        )
    ).astype(jnp.bfloat16)
    key_row_block = (
        frozen_key_base[0].astype(jnp.float32)
        + adapter_scale
        * jnp.dot(
            reduced_projection[:, adapter_depth : 2 * adapter_depth],
            key_value_up_weight[0],
            preferred_element_type=jnp.float32,
        )
    ).astype(jnp.bfloat16)
    value_row_block = (
        frozen_value_base[0].astype(jnp.float32)
        + adapter_scale
        * jnp.dot(
            reduced_projection[:, 2 * adapter_depth :],
            key_value_up_weight[1],
            preferred_element_type=jnp.float32,
        )
    ).astype(jnp.bfloat16)
    query_heads = query_rows.reshape(tok_count, kv_count, per_group, HEAD_SIZE)
    grad_heads = output_gradient[0].reshape(tok_count, kv_count, per_group, HEAD_SIZE)
    key_heads = key_row_block.reshape(tok_count, kv_count, HEAD_SIZE)
    value_heads = value_row_block.reshape(tok_count, kv_count, HEAD_SIZE)
    row_ids = lax.broadcasted_iota(jnp.int32, (tok_count, tok_count), 0)
    col_ids = lax.broadcasted_iota(jnp.int32, (tok_count, tok_count), 1)
    causal = col_ids <= row_ids
    straight = attend(
        query_heads[:, :, :half_heads],
        key_heads,
        value_heads,
        grad_heads[:, :, :half_heads],
        causal,
    )
    moved_queries = query_heads[:, :, half_heads:]
    moved_grads = grad_heads[:, :, half_heads:]
    earlier = shifted((key_heads[half_rows:], value_heads[half_rows:]), "context", 1)
    wide_keys = jnp.concatenate([earlier[0], key_heads], axis=0)
    wide_values = jnp.concatenate([earlier[1], value_heads], axis=0)
    wide_rows = lax.broadcasted_iota(jnp.int32, (tok_count, tok_count + half_rows), 0)
    wide_cols = lax.broadcasted_iota(jnp.int32, (tok_count, tok_count + half_rows), 1)
    lower_edge = jnp.where(wide_rows < half_rows, 0, tok_count)
    allowed = (wide_cols >= lower_edge) & (wide_cols <= wide_rows + half_rows)
    wide_parts = attend(moved_queries, wide_keys, wide_values, moved_grads, allowed)
    sent_back = shifted((wide_parts[2][:half_rows], wide_parts[3][:half_rows]), "context", -1)
    zero_rows = jnp.zeros_like(sent_back[0])
    moved_out = wide_parts[0]
    moved_dq = wide_parts[1]
    moved_dk = wide_parts[2][half_rows:] + jnp.concatenate([zero_rows, sent_back[0]], axis=0)
    moved_dv = wide_parts[3][half_rows:] + jnp.concatenate([zero_rows, sent_back[1]], axis=0)
    attended = (
        jnp.concatenate([straight[0], moved_out], axis=2)
        .reshape(tok_count, -1)
        .astype(jnp.bfloat16)
    )
    query_gradient = (
        jnp.concatenate([straight[1], moved_dq], axis=2).reshape(tok_count, -1).astype(jnp.bfloat16)
    )
    key_gradient = (straight[2] + moved_dk).reshape(tok_count, -1).astype(jnp.bfloat16)
    value_gradient = (straight[3] + moved_dv).reshape(tok_count, -1).astype(jnp.bfloat16)
    spanning_axis = (((0,), (0,)), ((), ()))
    query_adapter_gradient = adapter_scale * lax.dot_general(
        reduced_projection[:, :adapter_depth],
        query_gradient,
        spanning_axis,
        preferred_element_type=jnp.float32,
    )
    key_adapter_gradient = adapter_scale * lax.dot_general(
        reduced_projection[:, adapter_depth : 2 * adapter_depth],
        key_gradient,
        spanning_axis,
        preferred_element_type=jnp.float32,
    )
    value_adapter_gradient = adapter_scale * lax.dot_general(
        reduced_projection[:, 2 * adapter_depth :],
        value_gradient,
        spanning_axis,
        preferred_element_type=jnp.float32,
    )
    inner_product = (((1,), (1,)), ((), ()))
    outer = (((1,), (1,)), ((), ()))
    part = jnp.concatenate(
        [
            lax.dot_general(query_up_weight, query_gradient, outer, preferred_element_type=F32),
            lax.dot_general(
                key_value_up_weight[0], key_gradient, outer, preferred_element_type=F32
            ),
            lax.dot_general(
                key_value_up_weight[1], value_gradient, outer, preferred_element_type=F32
            ),
        ],
        axis=0,
    )
    down, up, pair = tail(
        part,
        token_count,
        query_adapter_gradient,
        jnp.concatenate([key_adapter_gradient, value_adapter_gradient], axis=0),
    )
    return (attended[None], down.T, up, pair.reshape(2, adapter_depth, -1))


def solution(mesh):
    split = Mesh(
        mesh.devices.reshape(2, 2, mesh.shape["context"], 2, 4),
        ("dp_0", "dp_1", "context", "tensor_0", "tensor_1"),
    )
    placed = (
        P(DP, "context", TENSOR),
        P(DP, "context", TENSOR),
        P(DP, "context", TENSOR),
        P(DP, "context", TENSOR),
        P(TENSOR, None),
        P(None, TENSOR),
        P(None, None, TENSOR),
        P(DP, "context", TENSOR),
    )
    return jax.shard_map(
        on_device,
        mesh=split,
        in_specs=placed,
        out_specs=(
            P(DP, "context", TENSOR),
            P(TENSOR, None),
            P(None, TENSOR),
            P(None, None, TENSOR),
        ),
        check_vma=False,
    )
```

```python
import jax
import jax.numpy as jnp
from jax import lax
from jax.experimental import pallas as pl
from jax.experimental.pallas import tpu as pltpu
from jax.sharding import Mesh
from jax.sharding import PartitionSpec as P

HEAD_SIZE = 128
TENSOR = ("tensor_0", "tensor_1")
DP = ("dp_0", "dp_1")
SCALE = HEAD_SIZE**-0.5
LOG2E = 1.4426950408889634
adapter_scale = 2.0

MESH_ID = pl.DeviceIdType.MESH
F32 = jnp.float32
BF16 = jnp.bfloat16
STEPS = (2, 1, -1, 0)
FAR = (4, 3, 5, 2, 6, 1, 7)


class Place:
    def __init__(self):
        self.x = lax.axis_index("dp_0")
        self.core = lax.axis_index("dp_1")
        self.z = lax.axis_index("context")
        self.half = lax.axis_index("tensor_0")
        self.y = lax.axis_index("tensor_1")
        self.depth = lax.axis_size("context")

    def near(self, a, b, step):
        z = lax.rem(self.z + step + self.depth, self.depth)
        return {
            "dp_0": lax.rem(self.x + a, 2),
            "dp_1": lax.rem(self.core + b, 2),
            "context": z,
        }

    def along(self, step):
        return {"context": lax.rem(self.z + step + self.depth, self.depth)}

    def chunk(self, a, b, step):
        x = lax.rem(self.x + a, 2)
        core = lax.rem(self.core + b, 2)
        return (x * 2 + core) * 4 + lax.rem(self.z + step + 4, 4)


def near_partners():
    for step in STEPS:
        for a in (1, 0):
            for b in (1, 0):
                if a or b or step:
                    yield a, b, step, (a * 2 + b) * 4 + STEPS.index(step)


def remote(src, dst, send_sem, recv_sem, device):
    return pltpu.make_async_remote_copy(
        src_ref=src,
        dst_ref=dst,
        send_sem=send_sem,
        recv_sem=recv_sem,
        device_id=device,
        device_id_type=MESH_ID,
    )


class TensorSum:
    def __init__(self, place, xs, xr, ys, yr, send, recv):
        self.xs, self.xr, self.ys, self.yr = xs, xr, ys, yr
        half = lax.rem(place.half + 1, 2)
        self.first = remote(xs, xr, send.at[0], recv.at[0], {"tensor_0": half})
        self.second = [
            remote(
                ys,
                yr.at[k - 1],
                send.at[k],
                recv.at[k],
                {"tensor_1": lax.rem(place.y + k, 4)},
            )
            for k in (2, 1, 3)
        ]

    def start(self, part):
        self.part = part
        self.xs[...] = part.astype(BF16)
        self.first.start()

    def middle(self):
        self.first.wait()
        self.total = self.part + self.xr[...].astype(F32)
        self.ys[...] = self.total.astype(BF16)
        for copy in self.second:
            copy.start()

    def end(self):
        for copy in self.second:
            copy.wait()
        total = self.total
        for k in range(3):
            total = total + self.yr[k].astype(F32)
        return total


class TokenSum:
    def __init__(self, place, mine, got, spread, full, send, recv):
        self.place = place
        self.mine, self.got, self.spread, self.full = mine, got, spread, full
        own = place.chunk(0, 0, 0)
        self.own = own
        self.group = place.z // 4
        groups = place.depth // 4
        self.first, self.third = [], []
        for a, b, step, slot in near_partners():
            device = place.near(a, b, step)
            self.first.append(
                (
                    slot,
                    remote(
                        mine.at[place.chunk(a, b, step)],
                        got.at[slot],
                        send.at[slot],
                        recv.at[slot],
                        device,
                    ),
                )
            )
            self.third.append(
                remote(
                    full.at[own], full.at[own], send.at[24 + slot], recv.at[24 + slot], device
                )
            )
        self.second = [
            remote(
                spread.at[self.group],
                spread.at[self.group],
                send.at[16 + k],
                recv.at[16 + k],
                place.along(4 * k),
            )
            for k in FAR
        ]
        self.groups = groups

    def start(self):
        for _, copy in self.first:
            copy.start()

    def middle(self):
        total = self.mine[self.own].astype(F32)
        for slot, copy in self.first:
            copy.wait_recv()
            total = total + self.got[slot].astype(F32)
        self.spread[self.group] = total.astype(BF16)
        for copy in self.second:
            copy.start()

    def late(self):
        for copy in self.second:
            copy.wait_recv()
        total = self.spread[0].astype(F32)
        for k in range(1, 8):
            total = total + self.spread[k].astype(F32)
        self.full[self.own] = total.astype(BF16)
        for copy in self.third:
            copy.start()

    def end(self):
        for copy in self.third:
            copy.wait_recv()

    def drain(self):
        for _, copy in self.first:
            copy.wait_send()
        for copy in self.second:
            copy.wait_send()
        for copy in self.third:
            copy.wait_send()


NN = (((1,), (0,)), ((), ()))
NT = (((1,), (1,)), ((), ()))
TN = (((0,), (0,)), ((), ()))


def mul(a, b, dims=NN):
    return lax.dot_general(a, b, dims, preferred_element_type=F32)


def greet(place):
    barrier = pltpu.get_barrier_semaphore()
    partners = []
    for step in (2, -2, 1, -1, 0):
        for a in (1, 0):
            for b in (1, 0):
                if a or b or step:
                    partners.append(place.near(a, b, step))
    partners.append({"tensor_0": lax.rem(place.half + 1, 2)})
    for k in (2, 1, 3):
        partners.append({"tensor_1": lax.rem(place.y + k, 4)})
    for device in partners:
        pl.semaphore_signal(barrier, inc=1, device_id=device, device_id_type=MESH_ID)
    return barrier, len(partners)


def tell(place, sem, step):
    for device in (place.along(step), place.along(-step)):
        pl.semaphore_signal(sem, inc=1, device_id=device, device_id_type=MESH_ID)


def kernel(
    normed_hbm,
    query_hbm,
    key_ref,
    value_ref,
    down_ref,
    up_ref,
    pair_ref,
    grad_hbm,
    attended_hbm,
    down_out,
    up_out,
    pair_out,
    normed,
    qs,
    dos,
    outs,
    kv,
    dkv,
    bias,
    rank_acc,
    up_acc,
    back_s,
    back_r,
    load_sem,
    store_sem,
    move_send,
    move_recv,
    reach,
    a_xs,
    a_xr,
    a_ys,
    a_yr,
    a_send,
    a_recv,
    d_xs,
    d_xr,
    d_ys,
    d_yr,
    d_send,
    d_recv,
    e_mine,
    e_got,
    e_spread,
    e_full,
    esend,
    erecv,
    g_mine,
    g_got,
    g_spread,
    g_full,
    gsend,
    grecv,
):
    place = Place()
    tokens = normed.shape[0]
    half = tokens // 2
    depth = up_ref.shape[0]
    heads = up_ref.shape[1] // HEAD_SIZE

    load = pltpu.make_async_copy(normed_hbm, normed, load_sem.at[0])
    load.start()
    loads = []
    for source, target, first in ((query_hbm, qs, 1), (grad_hbm, dos, 1 + 2 * heads)):
        for h in range(heads):
            for part in range(2):
                copy = pltpu.make_async_copy(
                    source.at[pl.ds(part * half, half), pl.ds(h * HEAD_SIZE, HEAD_SIZE)],
                    target.at[part, pl.ds(h * half, half), :],
                    load_sem.at[first + 2 * h + part],
                )
                copy.start()
                loads.append(copy)
    barrier, partners = greet(place)

    key_ids = lax.broadcasted_iota(jnp.int32, (half, tokens), 0)
    lanes = lax.broadcasted_iota(jnp.int32, (half, tokens), 1)
    row_ids = jnp.where(lanes < half, lanes, lanes - half)
    bias[...] = jnp.where(key_ids <= row_ids, 0.0, -jnp.inf)
    dkv[...] = jnp.zeros_like(dkv)
    rank_acc[...] = jnp.zeros_like(rank_acc)
    up_acc[...] = jnp.zeros_like(up_acc)

    early = TokenSum(place, e_mine, e_got, e_spread, e_full, esend, erecv)
    late = TokenSum(place, g_mine, g_got, g_spread, g_full, gsend, grecv)
    ranks = TensorSum(place, a_xs, a_xr, a_ys, a_yr, a_send, a_recv)
    rank_grads = TensorSum(place, d_xs, d_xr, d_ys, d_yr, d_send, d_recv)
    kv_out = remote(
        kv.at[:, pl.ds(tokens, half), :],
        kv.at[:, pl.ds(0, half), :],
        move_send.at[0],
        move_recv.at[0],
        place.along(1),
    )
    kv_back = remote(back_s, back_r, move_send.at[1], move_recv.at[1], place.along(-1))

    load.wait()
    low = mul(normed[...], down_ref[...])
    part = low.T
    pl.semaphore_wait(barrier, partners)
    ranks.start(part)
    tell(place, reach.at[0], 2)
    ranks.middle()
    pl.semaphore_wait(reach.at[0], 2)
    tell(place, reach.at[1], 4)
    low_t = ranks.end()
    low_bf = low_t.astype(BF16)
    low_rows = low_bf.astype(F32).T.astype(BF16)
    pl.semaphore_wait(reach.at[1], 2)
    tell(place, reach.at[2], 8)

    for i, base in enumerate((key_ref, value_ref)):
        lows = low_rows[:, depth * (i + 1) : depth * (i + 2)]
        kv[i, half:, :] = (base[...].astype(F32) + adapter_scale * mul(lows, pair_ref[i])).astype(
            BF16
        )
    kv_out.start()

    for copy in loads:
        copy.wait()
    query_low = low_rows[:, :depth]
    for h in range(heads):
        step = adapter_scale * mul(query_low, up_ref[:, h * HEAD_SIZE : (h + 1) * HEAD_SIZE])
        for p in range(2):
            rows = slice(h * half, (h + 1) * half)
            qs[p, rows, :] = (
                qs[p, rows, :].astype(F32) + step[p * half : (p + 1) * half]
            ).astype(BF16)

    low_q = low_bf[:depth].astype(F32)
    turned = pltpu.roll(low_q, half, 1)
    in_first = lax.broadcasted_iota(jnp.int32, low_q.shape, 1) < half
    zero = jnp.zeros_like(low_q)
    wide_low = (
        jnp.concatenate(
            [jnp.where(in_first, low_q, zero), jnp.where(in_first, zero, turned)], axis=0
        ).astype(BF16),
        jnp.concatenate(
            [jnp.where(in_first, turned, zero), jnp.where(in_first, zero, low_q)], axis=0
        ).astype(BF16),
    )

    stores = []

    def unit(first, count, p, pair):
        rows = slice(pair * tokens, (pair + 1) * tokens)
        keys = kv[0, first : first + count, :]
        values = kv[1, first : first + count, :]
        queries = qs[p, rows, :]
        grads = dos[p, rows, :]
        scores = mul(keys, queries, NT) * (SCALE * LOG2E)
        if count > half:
            scores = jnp.concatenate([scores[:half], scores[half:] + bias[...]], axis=0)
        else:
            scores = scores + bias[...]
        highest = jnp.max(scores, axis=0, keepdims=True)
        weights = jnp.exp2(scores - highest)
        probs = weights * (1.0 / jnp.sum(weights, axis=0, keepdims=True))
        probs_low = probs.astype(BF16)
        prob_grad = mul(values, grads, NT)
        row_dot = jnp.sum(probs * prob_grad, axis=0, keepdims=True)
        score_grad = (probs * (prob_grad - row_dot) * SCALE).astype(BF16)
        outs[p, rows, :] = mul(values, probs_low, TN).T.astype(BF16)
        query_grad = mul(keys, score_grad, TN).astype(BF16)
        dkv[0, first : first + count, :] += mul(score_grad, queries)
        dkv[1, first : first + count, :] += mul(probs_low, grads)
        one, two = 2 * pair, 2 * pair + 1
        ups = jnp.concatenate(
            [up_ref[:, h * HEAD_SIZE : (h + 1) * HEAD_SIZE] for h in (one, two)], axis=0
        )
        rank_acc[p] += mul(ups, query_grad)
        up_acc[pair] += mul(wide_low[p], query_grad, NT)
        for h in (one, two):
            copy = pltpu.make_async_copy(
                outs.at[p, pl.ds(h * half, half), :],
                attended_hbm.at[pl.ds(p * half, half), pl.ds(h * HEAD_SIZE, HEAD_SIZE)],
                store_sem.at[2 * h + p],
            )
            copy.start()
            stores.append(copy)

    unit(half, tokens, 1, 0)
    unit(half, tokens, 1, 1)
    unit(half, half, 0, 0)
    kv_out.wait()
    unit(0, tokens, 0, 2)
    unit(0, tokens, 0, 3)
    back_s[...] = dkv[:, :half, :].astype(BF16)
    kv_back.start()
    unit(half, half, 0, 1)
    unit(tokens, half, 1, 2)
    unit(tokens, half, 1, 3)

    first, second = rank_acc[0], rank_acc[1]
    ours = first[:depth] + pltpu.roll(first[depth:], half, 1)
    theirs = pltpu.roll(second[:depth], half, 1) + second[depth:]
    query_part = jnp.where(in_first, ours, theirs)
    kv_back.wait()
    dkv[:, tokens:, :] += back_r[...].astype(F32)
    parts, pair_grads = [query_part], []
    for i in range(2):
        grad = dkv[i, half:, :].astype(BF16)
        parts.append(mul(pair_ref[i], grad, NT))
        pair_grads.append(adapter_scale * mul(low_bf[depth * (i + 1) : depth * (i + 2)], grad))
    rank_grads.start(jnp.concatenate(parts, axis=0))
    zeros = jnp.zeros((8, 128), F32)
    for c in range(16):
        h, q = c // 2, c % 2
        top = 16 * (h % 2) + 8 * q
        upper = adapter_scale * up_acc[h // 2, top : top + 8, :]
        lower = pair_grads[c // 2][8 * q : 8 * q + 8] if c < 4 else zeros
        e_mine[c] = jnp.concatenate([upper, lower], axis=0).astype(BF16)
    early.start()
    rank_grads.middle()
    pl.semaphore_wait(reach.at[2], 2)
    early.middle()
    rank_grad = (adapter_scale * rank_grads.end()).astype(BF16)
    for j in range(8):
        columns = slice(128 * j, 128 * j + 128)
        down = mul(rank_grad, normed[:, columns])
        g_mine[2 * j] = down[:24].astype(BF16)
        g_mine[2 * j + 1] = down[24:].astype(BF16)
    late.start()
    late.middle()
    early.late()
    early.end()
    for c in range(16):
        value = e_full[c].astype(F32)
        up_out[8 * (c % 2) : 8 * (c % 2) + 8, 128 * (c // 2) : 128 * (c // 2) + 128] = value[:8]
        if c < 4:
            pair_out[8 * c : 8 * c + 8, :] = value[8:]
    late.late()
    late.end()
    for c in range(16):
        down_out[24 * (c % 2) : 24 * (c % 2) + 24, 128 * (c // 2) : 128 * (c // 2) + 128] = g_full[
            c
        ].astype(F32)
    for copy in stores:
        copy.wait()
    early.drain()
    late.drain()


def token_sum_scratch(rows):
    return [
        pltpu.VMEM((16, rows, 128), BF16),
        pltpu.VMEM((16, rows, 128), BF16),
        pltpu.VMEM((8, rows, 128), BF16),
        pltpu.VMEM((16, rows, 128), BF16),
        pltpu.SemaphoreType.DMA((40,)),
        pltpu.SemaphoreType.DMA((40,)),
    ]


def tensor_sum_scratch(ranks, tokens):
    return [
        pltpu.VMEM((ranks, tokens), BF16),
        pltpu.VMEM((ranks, tokens), BF16),
        pltpu.VMEM((ranks, tokens), BF16),
        pltpu.VMEM((3, ranks, tokens), BF16),
        pltpu.SemaphoreType.DMA((4,)),
        pltpu.SemaphoreType.DMA((4,)),
    ]


def on_device(normed, query_base, key_base, value_base, down, up, pair, grad):
    vmem = pl.BlockSpec(memory_space=pltpu.VMEM)
    hbm = pl.BlockSpec(memory_space=pl.ANY)
    tokens, width = normed.shape[1:]
    depth = up.shape[0]
    ranks = down.shape[1]
    heads = width // HEAD_SIZE
    half = tokens // 2
    stacked = (2, heads * half, HEAD_SIZE)
    attended, down_grad, up_grad, pair_grad = pl.pallas_call(
        kernel,
        out_shape=(
            jax.ShapeDtypeStruct((tokens, width), BF16),
            jax.ShapeDtypeStruct((ranks, width), F32),
            jax.ShapeDtypeStruct((depth, width), F32),
            jax.ShapeDtypeStruct((2 * depth, HEAD_SIZE), F32),
        ),
        in_specs=[hbm, hbm, vmem, vmem, vmem, vmem, vmem, hbm],
        out_specs=(hbm, vmem, vmem, vmem),
        scratch_shapes=[
            pltpu.VMEM((tokens, width), BF16),
            pltpu.VMEM(stacked, BF16),
            pltpu.VMEM(stacked, BF16),
            pltpu.VMEM(stacked, BF16),
            pltpu.VMEM((2, tokens + half, HEAD_SIZE), BF16),
            pltpu.VMEM((2, tokens + half, HEAD_SIZE), F32),
            pltpu.VMEM((half, tokens), F32),
            pltpu.VMEM((2, 2 * depth, tokens), F32),
            pltpu.VMEM((heads // 2, 2 * depth, HEAD_SIZE), F32),
            pltpu.VMEM((2, half, HEAD_SIZE), BF16),
            pltpu.VMEM((2, half, HEAD_SIZE), BF16),
            pltpu.SemaphoreType.DMA((1 + 4 * heads,)),
            pltpu.SemaphoreType.DMA((2 * heads,)),
            pltpu.SemaphoreType.DMA((2,)),
            pltpu.SemaphoreType.DMA((2,)),
            pltpu.SemaphoreType.REGULAR((3,)),
        ]
        + tensor_sum_scratch(ranks, tokens)
        + tensor_sum_scratch(ranks, tokens)
        + token_sum_scratch(16)
        + token_sum_scratch(24),
        compiler_params=pltpu.CompilerParams(
            collective_id=0, has_side_effects=True, vmem_limit_bytes=56 * 1024 * 1024
        ),
    )(normed[0], query_base[0], key_base[0], value_base[0], down, up, pair, grad[0])
    return (attended[None], down_grad.T, up_grad, pair_grad.reshape(2, depth, -1))


def solution(mesh):
    split = Mesh(
        mesh.devices.reshape(2, 2, mesh.shape["context"], 2, 4),
        ("dp_0", "dp_1", "context", "tensor_0", "tensor_1"),
    )
    placed = (
        P(DP, "context", TENSOR),
        P(DP, "context", TENSOR),
        P(DP, "context", TENSOR),
        P(DP, "context", TENSOR),
        P(TENSOR, None),
        P(None, TENSOR),
        P(None, None, TENSOR),
        P(DP, "context", TENSOR),
    )
    return jax.shard_map(
        on_device,
        mesh=split,
        in_specs=placed,
        out_specs=(
            P(DP, "context", TENSOR),
            P(TENSOR, None),
            P(None, TENSOR),
            P(None, None, TENSOR),
        ),
        check_vma=False,
    )
```

```python
import jax
import jax.numpy as jnp
from jax import lax
from jax.experimental import pallas as pl
from jax.experimental.pallas import tpu as pltpu
from jax.sharding import Mesh
from jax.sharding import PartitionSpec as P

HEAD_SIZE = 128
TENSOR = ("tensor_0", "tensor_1")
DP = ("dp_0", "dp_1")
SCALE = HEAD_SIZE**-0.5
LOG2E = 1.4426950408889634
adapter_scale = 2.0

MESH_ID = pl.DeviceIdType.MESH
F32 = jnp.float32
BF16 = jnp.bfloat16
STEPS = (2, 1, -1, 0)
FAR = (4, 3, 5, 2, 6, 1, 7)


class Place:
    def __init__(self):
        self.x = lax.axis_index("dp_0")
        self.core = lax.axis_index("dp_1")
        self.z = lax.axis_index("context")
        self.half = lax.axis_index("tensor_0")
        self.y = lax.axis_index("tensor_1")
        self.depth = lax.axis_size("context")

    def near(self, a, b, step):
        z = lax.rem(self.z + step + self.depth, self.depth)
        return {
            "dp_0": lax.rem(self.x + a, 2),
            "dp_1": lax.rem(self.core + b, 2),
            "context": z,
        }

    def along(self, step):
        return {"context": lax.rem(self.z + step + self.depth, self.depth)}

    def chunk(self, a, b, step):
        x = lax.rem(self.x + a, 2)
        core = lax.rem(self.core + b, 2)
        return (x * 2 + core) * 4 + lax.rem(self.z + step + 4, 4)


def near_partners():
    for step in STEPS:
        for a in (1, 0):
            for b in (1, 0):
                if a or b or step:
                    yield a, b, step, (a * 2 + b) * 4 + STEPS.index(step)


def remote(src, dst, send_sem, recv_sem, device):
    return pltpu.make_async_remote_copy(
        src_ref=src,
        dst_ref=dst,
        send_sem=send_sem,
        recv_sem=recv_sem,
        device_id=device,
        device_id_type=MESH_ID,
    )


class TensorSum:
    def __init__(self, place, xs, xr, ys, yr, send, recv):
        self.xs, self.xr, self.ys, self.yr = xs, xr, ys, yr
        half = lax.rem(place.half + 1, 2)
        chunks = range(xs.shape[0])
        self.first = [
            remote(
                xs.at[c], xr.at[c], send.at[4 * c], recv.at[4 * c], {"tensor_0": half}
            )
            for c in chunks
        ]
        self.second = [
            [
                remote(
                    ys.at[c],
                    yr.at[c, k - 1],
                    send.at[4 * c + k],
                    recv.at[4 * c + k],
                    {"tensor_1": lax.rem(place.y + k, 4)},
                )
                for k in (2, 1, 3)
            ]
            for c in chunks
        ]
        self.part, self.total = {}, {}

    def start(self, c, part):
        self.part[c] = part
        self.xs[c] = part.astype(BF16)
        self.first[c].start()

    def middle(self, c):
        self.first[c].wait()
        self.total[c] = self.part[c] + self.xr[c].astype(F32)
        self.ys[c] = self.total[c].astype(BF16)
        for copy in self.second[c]:
            copy.start()

    def end(self, c):
        for copy in self.second[c]:
            copy.wait()
        total = self.total[c]
        for k in range(3):
            total = total + self.yr[c, k].astype(F32)
        return total


class TokenSum:
    def __init__(self, place, mine, got, spread, full, send, recv):
        self.place = place
        self.mine, self.got, self.spread, self.full = mine, got, spread, full
        own = place.chunk(0, 0, 0)
        self.own = own
        self.group = place.z // 4
        groups = place.depth // 4
        self.first, self.third = [], []
        for a, b, step, slot in near_partners():
            device = place.near(a, b, step)
            self.first.append(
                (
                    slot,
                    remote(
                        mine.at[place.chunk(a, b, step)],
                        got.at[slot],
                        send.at[slot],
                        recv.at[slot],
                        device,
                    ),
                )
            )
            self.third.append(
                remote(
                    full.at[own], full.at[own], send.at[24 + slot], recv.at[24 + slot], device
                )
            )
        self.second = [
            remote(
                spread.at[self.group],
                spread.at[self.group],
                send.at[16 + k],
                recv.at[16 + k],
                place.along(4 * k),
            )
            for k in FAR
        ]
        self.groups = groups

    def start(self):
        for _, copy in self.first:
            copy.start()

    def middle(self):
        total = self.mine[self.own].astype(F32)
        for slot, copy in self.first:
            copy.wait_recv()
            total = total + self.got[slot].astype(F32)
        self.spread[self.group] = total.astype(BF16)
        for copy in self.second:
            copy.start()

    def late(self):
        for copy in self.second:
            copy.wait_recv()
        total = self.spread[0].astype(F32)
        for k in range(1, 8):
            total = total + self.spread[k].astype(F32)
        self.full[self.own] = total.astype(BF16)
        for copy in self.third:
            copy.start()

    def end(self):
        for copy in self.third:
            copy.wait_recv()

    def drain(self):
        for _, copy in self.first:
            copy.wait_send()
        for copy in self.second:
            copy.wait_send()
        for copy in self.third:
            copy.wait_send()


NN = (((1,), (0,)), ((), ()))
NT = (((1,), (1,)), ((), ()))
TN = (((0,), (0,)), ((), ()))


def mul(a, b, dims=NN):
    return lax.dot_general(a, b, dims, preferred_element_type=F32)


def greet(place):
    barrier = pltpu.get_barrier_semaphore()
    partners = []
    for step in (2, -2, 1, -1, 0):
        for a in (1, 0):
            for b in (1, 0):
                if a or b or step:
                    partners.append(place.near(a, b, step))
    partners.append({"tensor_0": lax.rem(place.half + 1, 2)})
    for k in (2, 1, 3):
        partners.append({"tensor_1": lax.rem(place.y + k, 4)})
    for device in partners:
        pl.semaphore_signal(barrier, inc=1, device_id=device, device_id_type=MESH_ID)
    return barrier, len(partners)


def tell(place, sem, step):
    for device in (place.along(step), place.along(-step)):
        pl.semaphore_signal(sem, inc=1, device_id=device, device_id_type=MESH_ID)


def kernel(
    normed_hbm,
    query_hbm,
    key_hbm,
    value_hbm,
    down_hbm,
    up_hbm,
    pair_hbm,
    grad_hbm,
    outs,
    down_out,
    up_out,
    pair_out,
    normed,
    qs,
    dos,
    base,
    down_ref,
    up_ref,
    pair_ref,
    kv,
    dkv,
    bias,
    rank_acc,
    up_acc,
    low_s,
    low_r,
    base_r,
    back_s,
    back_r,
    load_sem,
    move_send,
    move_recv,
    reach,
    a_xs,
    a_xr,
    a_ys,
    a_yr,
    a_send,
    a_recv,
    d_xs,
    d_xr,
    d_ys,
    d_yr,
    d_send,
    d_recv,
    e_mine,
    e_got,
    e_spread,
    e_full,
    esend,
    erecv,
    g_mine,
    g_got,
    g_spread,
    g_full,
    gsend,
    grecv,
):
    place = Place()
    tokens, width = normed.shape
    half = tokens // 2
    depth = up_ref.shape[0]
    heads = up_ref.shape[1] // HEAD_SIZE
    tail = low_r.shape[2]
    pad = tail - half

    index = 0

    def fetch(source, target):
        nonlocal index
        copy = pltpu.make_async_copy(source, target, load_sem.at[index])
        copy.start()
        index += 1
        return copy

    down_load = fetch(down_hbm, down_ref)
    halves = [pl.ds(k * (width // 2), width // 2) for k in range(2)]
    normed_loads = [fetch(normed_hbm.at[:, k], normed.at[:, k]) for k in halves]
    base_loads = [fetch(key_hbm, base.at[0]), fetch(value_hbm, base.at[1])]
    weight_loads = [fetch(pair_hbm, pair_ref), fetch(up_hbm, up_ref)]
    loads = []
    for source, target in ((query_hbm, qs), (grad_hbm, dos)):
        for h in range(heads):
            for p in range(2):
                loads.append(
                    fetch(
                        source.at[pl.ds(p * half, half), pl.ds(h * HEAD_SIZE, HEAD_SIZE)],
                        target.at[p, pl.ds(h * half, half), :],
                    )
                )
    barrier, partners = greet(place)

    early = TokenSum(place, e_mine, e_got, e_spread, e_full, esend, erecv)
    late = TokenSum(place, g_mine, g_got, g_spread, g_full, gsend, grecv)
    ranks = TensorSum(place, a_xs, a_xr, a_ys, a_yr, a_send, a_recv)
    rank_grads = TensorSum(place, d_xs, d_xr, d_ys, d_yr, d_send, d_recv)
    base_out = remote(
        base.at[:, pl.ds(half, half), :], base_r, move_send.at[0], move_recv.at[0], place.along(1)
    )
    low_out = [
        remote(
            low_s.at[i, :, pl.ds(tokens - tail, tail)],
            low_r.at[i],
            move_send.at[1 + i],
            move_recv.at[1 + i],
            place.along(1),
        )
        for i in range(2)
    ]
    back = remote(back_s, back_r, move_send.at[3], move_recv.at[3], place.along(-1))

    down_load.wait()
    low = None
    for k, copy in enumerate(normed_loads):
        copy.wait()
        columns = slice(k * (width // 2), (k + 1) * (width // 2))
        term = mul(down_ref[:, columns], normed[:, columns], NT)
        low = term if low is None else low + term
    pl.semaphore_wait(barrier, partners)
    for c in (1, 2, 0):
        ranks.start(c, low[depth * c : depth * (c + 1)])
    for copy in base_loads:
        copy.wait()
    base_out.start()
    tell(place, reach.at[0], 2)

    key_ids = lax.broadcasted_iota(jnp.int32, (half, tokens), 0)
    lanes = lax.broadcasted_iota(jnp.int32, (half, tokens), 1)
    row_ids = jnp.where(lanes < half, lanes, lanes - half)
    bias[...] = jnp.where(key_ids <= row_ids, 0.0, -jnp.inf)
    dkv[...] = jnp.zeros_like(dkv)
    rank_acc[...] = jnp.zeros_like(rank_acc)
    up_acc[...] = jnp.zeros_like(up_acc)

    for c in (1, 2, 0):
        ranks.middle(c)
    pl.semaphore_wait(reach.at[0], 2)
    tell(place, reach.at[1], 4)
    for copy in weight_loads:
        copy.wait()
    for i in range(2):
        low_s[i] = ranks.end(1 + i).astype(BF16)
        low_out[i].start()
        kv[i, half:, :] = (
            base[i].astype(F32) + adapter_scale * mul(low_s[i], pair_ref[i], TN)
        ).astype(BF16)
    low_q = ranks.end(0).astype(BF16)
    low_q32 = low_q.astype(F32)
    query_low = low_q32.T.astype(BF16)
    for copy in loads:
        copy.wait()
    for h in range(heads):
        step = adapter_scale * mul(query_low, up_ref[:, h * HEAD_SIZE : (h + 1) * HEAD_SIZE])
        for p in range(2):
            rows = slice(h * half, (h + 1) * half)
            qs[p, rows, :] = (
                qs[p, rows, :].astype(F32) + step[p * half : (p + 1) * half]
            ).astype(BF16)

    turned = pltpu.roll(low_q32, half, 1)
    in_first = lax.broadcasted_iota(jnp.int32, low_q.shape, 1) < half
    zero = jnp.zeros_like(low_q32)
    wide_low = (
        jnp.concatenate(
            [jnp.where(in_first, low_q32, zero), jnp.where(in_first, zero, turned)], axis=0
        ).astype(BF16),
        jnp.concatenate(
            [jnp.where(in_first, turned, zero), jnp.where(in_first, zero, low_q32)], axis=0
        ).astype(BF16),
    )

    def unit(first, count, p, pair):
        rows = slice(pair * tokens, (pair + 1) * tokens)
        keys = kv[0, first : first + count, :]
        values = kv[1, first : first + count, :]
        queries = qs[p, rows, :]
        grads = dos[p, rows, :]
        scores = mul(keys, queries, NT) * (SCALE * LOG2E)
        if count > half:
            scores = jnp.concatenate([scores[:half], scores[half:] + bias[...]], axis=0)
        else:
            scores = scores + bias[...]
        highest = jnp.max(scores, axis=0, keepdims=True)
        weights = jnp.exp2(scores - highest)
        probs = weights * (1.0 / jnp.sum(weights, axis=0, keepdims=True))
        probs_low = probs.astype(BF16)
        prob_grad = mul(values, grads, NT)
        row_dot = jnp.sum(probs * prob_grad, axis=0, keepdims=True)
        score_grad = (probs * (prob_grad - row_dot) * SCALE).astype(BF16)
        outs[p, rows, :] = mul(values, probs_low, TN).T.astype(BF16)
        query_grad = mul(keys, score_grad, TN).astype(BF16)
        dkv[0, pad + first : pad + first + count, :] += mul(score_grad, queries)
        dkv[1, pad + first : pad + first + count, :] += mul(probs_low, grads)
        one, two = 2 * pair, 2 * pair + 1
        ups = jnp.concatenate(
            [up_ref[:, h * HEAD_SIZE : (h + 1) * HEAD_SIZE] for h in (one, two)], axis=0
        )
        rank_acc[p] += mul(ups, query_grad)
        up_acc[pair] += mul(wide_low[p], query_grad, NT)

    unit(half, tokens, 1, 0)
    unit(half, tokens, 1, 1)
    base_out.wait()
    for i in range(2):
        low_out[i].wait()
        step = adapter_scale * mul(low_r[i], pair_ref[i], TN)
        kv[i, :half, :] = (base_r[i].astype(F32) + step[pad:]).astype(BF16)
    unit(0, tokens, 0, 2)
    unit(0, tokens, 0, 3)
    far_grads = [dkv[i, :tail, :].astype(BF16) for i in range(2)]
    for i in range(2):
        back_s[i] = mul(pair_ref[i], far_grads[i], NT).astype(BF16)
    back.start()
    unit(half, half, 0, 0)
    unit(half, half, 0, 1)
    unit(tokens, half, 1, 2)
    unit(tokens, half, 1, 3)

    first, second = rank_acc[0], rank_acc[1]
    ours = first[:depth] + pltpu.roll(first[depth:], half, 1)
    theirs = pltpu.roll(second[:depth], half, 1) + second[depth:]
    rank_grads.start(0, jnp.where(in_first, ours, theirs))
    grads = [dkv[i, tail:, :].astype(BF16) for i in range(2)]
    parts = [mul(pair_ref[i], grads[i], NT) for i in range(2)]
    back.wait()
    for i in range(2):
        near = parts[i][:, : tokens - tail]
        far = parts[i][:, tokens - tail :] + back_r[i].astype(F32)
        rank_grads.start(1 + i, jnp.concatenate([near, far], axis=1))
    pair_grads = [
        adapter_scale * (mul(low_s[i], grads[i]) + mul(low_r[i], far_grads[i])) for i in range(2)
    ]
    zeros = jnp.zeros((8, 128), F32)
    for c in range(16):
        h, q = c // 2, c % 2
        top = 16 * (h % 2) + 8 * q
        upper = adapter_scale * up_acc[h // 2, top : top + 8, :]
        lower = pair_grads[c // 2][8 * q : 8 * q + 8] if c < 4 else zeros
        e_mine[c] = jnp.concatenate([upper, lower], axis=0).astype(BF16)
    for c in range(3):
        rank_grads.middle(c)
    early.start()
    pl.semaphore_wait(reach.at[1], 2)
    tell(place, reach.at[2], 8)
    rank_grad = jnp.concatenate(
        [(adapter_scale * rank_grads.end(c)).astype(BF16) for c in range(3)], axis=0
    )
    for j in range(8):
        columns = slice(128 * j, 128 * j + 128)
        down = mul(rank_grad, normed[:, columns])
        g_mine[2 * j] = down[:24].astype(BF16)
        g_mine[2 * j + 1] = down[24:].astype(BF16)
    late.start()
    pl.semaphore_wait(reach.at[2], 2)
    early.middle()
    late.middle()
    early.late()
    early.end()
    for c in range(16):
        value = e_full[c].astype(F32)
        up_out[8 * (c % 2) : 8 * (c % 2) + 8, 128 * (c // 2) : 128 * (c // 2) + 128] = value[:8]
        if c < 4:
            pair_out[8 * c : 8 * c + 8, :] = value[8:]
    late.late()
    late.end()
    for c in range(16):
        down_out[24 * (c % 2) : 24 * (c % 2) + 24, 128 * (c // 2) : 128 * (c // 2) + 128] = g_full[
            c
        ].astype(F32)
    early.drain()
    late.drain()


def store_kernel(outs, down, up, pair, attended_hbm, down_hbm, up_hbm, pair_hbm, sem):
    half = attended_hbm.shape[0] // 2
    heads = attended_hbm.shape[1] // HEAD_SIZE
    copies = [
        pltpu.make_async_copy(
            outs.at[p, pl.ds(h * half, half), :],
            attended_hbm.at[pl.ds(p * half, half), pl.ds(h * HEAD_SIZE, HEAD_SIZE)],
            sem.at[2 * h + p],
        )
        for h in range(heads)
        for p in range(2)
    ]
    for k, (source, target) in enumerate(((down, down_hbm), (up, up_hbm), (pair, pair_hbm))):
        copies.append(pltpu.make_async_copy(source, target, sem.at[2 * heads + k]))
    for copy in copies:
        copy.start()
    for copy in copies:
        copy.wait()


def token_sum_scratch(rows):
    return [
        pltpu.VMEM((16, rows, 128), BF16),
        pltpu.VMEM((16, rows, 128), BF16),
        pltpu.VMEM((8, rows, 128), BF16),
        pltpu.VMEM((16, rows, 128), BF16),
        pltpu.SemaphoreType.DMA((40,)),
        pltpu.SemaphoreType.DMA((40,)),
    ]


def tensor_sum_scratch(chunks, rows, tokens):
    return [
        pltpu.VMEM((chunks, rows, tokens), BF16),
        pltpu.VMEM((chunks, rows, tokens), BF16),
        pltpu.VMEM((chunks, rows, tokens), BF16),
        pltpu.VMEM((chunks, 3, rows, tokens), BF16),
        pltpu.SemaphoreType.DMA((4 * chunks,)),
        pltpu.SemaphoreType.DMA((4 * chunks,)),
    ]


def on_device(normed, query_base, key_base, value_base, down, up, pair, grad):
    vmem = pl.BlockSpec(memory_space=pltpu.VMEM)
    hbm = pl.BlockSpec(memory_space=pltpu.HBM)
    tokens, width = normed.shape[1:]
    depth = up.shape[0]
    ranks = down.shape[1]
    heads = width // HEAD_SIZE
    half = tokens // 2
    tail = 256
    stacked = (2, heads * half, HEAD_SIZE)
    results = pl.pallas_call(
        kernel,
        out_shape=(
            pltpu.VMEM(stacked, BF16),
            pltpu.VMEM((ranks, width), F32),
            pltpu.VMEM((depth, width), F32),
            pltpu.VMEM((2 * depth, HEAD_SIZE), F32),
        ),
        in_specs=[hbm] * 8,
        out_specs=(vmem,) * 4,
        scratch_shapes=[
            pltpu.VMEM((tokens, width), BF16),
            pltpu.VMEM(stacked, BF16),
            pltpu.VMEM(stacked, BF16),
            pltpu.VMEM((2, tokens, HEAD_SIZE), BF16),
            pltpu.VMEM((ranks, width), BF16),
            pltpu.VMEM((depth, width), BF16),
            pltpu.VMEM((2, depth, HEAD_SIZE), BF16),
            pltpu.VMEM((2, tokens + half, HEAD_SIZE), BF16),
            pltpu.VMEM((2, tokens + tail, HEAD_SIZE), F32),
            pltpu.VMEM((half, tokens), F32),
            pltpu.VMEM((2, 2 * depth, tokens), F32),
            pltpu.VMEM((heads // 2, 2 * depth, HEAD_SIZE), F32),
            pltpu.VMEM((2, depth, tokens), BF16),
            pltpu.VMEM((2, depth, tail), BF16),
            pltpu.VMEM((2, half, HEAD_SIZE), BF16),
            pltpu.VMEM((2, depth, tail), BF16),
            pltpu.VMEM((2, depth, tail), BF16),
            pltpu.SemaphoreType.DMA((7 + 4 * heads,)),
            pltpu.SemaphoreType.DMA((4,)),
            pltpu.SemaphoreType.DMA((4,)),
            pltpu.SemaphoreType.REGULAR((3,)),
        ]
        + tensor_sum_scratch(3, depth, tokens)
        + tensor_sum_scratch(3, depth, tokens)
        + token_sum_scratch(16)
        + token_sum_scratch(24),
        compiler_params=pltpu.CompilerParams(
            collective_id=0, has_side_effects=True, vmem_limit_bytes=60 * 1024 * 1024
        ),
    )(normed[0], query_base[0], key_base[0], value_base[0], down.T, up, pair, grad[0])
    attended, down_grad, up_grad, pair_grad = pl.pallas_call(
        store_kernel,
        out_shape=(
            jax.ShapeDtypeStruct((tokens, width), BF16),
            jax.ShapeDtypeStruct((ranks, width), F32),
            jax.ShapeDtypeStruct((depth, width), F32),
            jax.ShapeDtypeStruct((2 * depth, HEAD_SIZE), F32),
        ),
        in_specs=[vmem] * 4,
        out_specs=(hbm,) * 4,
        scratch_shapes=[pltpu.SemaphoreType.DMA((2 * heads + 3,))],
        compiler_params=pltpu.CompilerParams(vmem_limit_bytes=1024 * 1024),
    )(*results)
    return (attended[None], down_grad.T, up_grad, pair_grad.reshape(2, depth, -1))


def solution(mesh):
    split = Mesh(
        mesh.devices.reshape(2, 2, mesh.shape["context"], 2, 4),
        ("dp_0", "dp_1", "context", "tensor_0", "tensor_1"),
    )
    placed = (
        P(DP, "context", TENSOR),
        P(DP, "context", TENSOR),
        P(DP, "context", TENSOR),
        P(DP, "context", TENSOR),
        P(TENSOR, None),
        P(None, TENSOR),
        P(None, None, TENSOR),
        P(DP, "context", TENSOR),
    )
    return jax.shard_map(
        on_device,
        mesh=split,
        in_specs=placed,
        out_specs=(
            P(DP, "context", TENSOR),
            P(TENSOR, None),
            P(None, TENSOR),
            P(None, None, TENSOR),
        ),
        check_vma=False,
    )
```

```python
import jax
import jax.numpy as jnp
from jax import lax
from jax.experimental import pallas as pl
from jax.experimental.pallas import tpu as pltpu
from jax.sharding import Mesh
from jax.sharding import PartitionSpec as P

HEAD_SIZE = 128
TENSOR = ("tensor_0", "tensor_1")
DP = ("dp_0", "dp_1")
SCALE = HEAD_SIZE**-0.5
LOG2E = 1.4426950408889634
adapter_scale = 2.0

MESH_ID = pl.DeviceIdType.MESH
F32 = jnp.float32
BF16 = jnp.bfloat16
STEPS = (2, 1, -1, 0)
FAR = (4, 3, 5, 2, 6, 1, 7)
STORES = 4


class Place:
    def __init__(self):
        self.x = lax.axis_index("dp_0")
        self.core = lax.axis_index("dp_1")
        self.z = lax.axis_index("context")
        self.half = lax.axis_index("tensor_0")
        self.y = lax.axis_index("tensor_1")
        self.depth = lax.axis_size("context")

    def near(self, a, b, step):
        z = lax.rem(self.z + step + self.depth, self.depth)
        return {
            "dp_0": lax.rem(self.x + a, 2),
            "dp_1": lax.rem(self.core + b, 2),
            "context": z,
        }

    def along(self, step):
        return {"context": lax.rem(self.z + step + self.depth, self.depth)}

    def chunk(self, a, b, step):
        x = lax.rem(self.x + a, 2)
        core = lax.rem(self.core + b, 2)
        return (x * 2 + core) * 4 + lax.rem(self.z + step + 4, 4)


def near_partners():
    for i, step in enumerate(STEPS):
        for a in (1, 0):
            for b in (1, 0):
                if a or b or step:
                    yield a, b, (-step if step == 2 and b else step), (a * 2 + b) * 4 + i


def remote(src, dst, send_sem, recv_sem, device):
    return pltpu.make_async_remote_copy(
        src_ref=src,
        dst_ref=dst,
        send_sem=send_sem,
        recv_sem=recv_sem,
        device_id=device,
        device_id_type=MESH_ID,
    )


class TensorSum:
    def __init__(self, place, xs, xr, ys, yr, send, recv):
        self.xs, self.xr, self.ys, self.yr = xs, xr, ys, yr
        half = lax.rem(place.half + 1, 2)
        chunks = range(xs.shape[0])
        self.first = [
            remote(
                xs.at[c], xr.at[c], send.at[4 * c], recv.at[4 * c], {"tensor_0": half}
            )
            for c in chunks
        ]
        self.second = [
            [
                remote(
                    ys.at[c],
                    yr.at[c, k - 1],
                    send.at[4 * c + k],
                    recv.at[4 * c + k],
                    {"tensor_1": lax.rem(place.y + k, 4)},
                )
                for k in (2, 1, 3)
            ]
            for c in chunks
        ]
        self.part, self.total = {}, {}

    def start(self, c, part):
        self.part[c] = part
        self.xs[c] = part.astype(BF16)
        self.first[c].start()

    def middle(self, c):
        self.first[c].wait()
        self.total[c] = self.part[c] + self.xr[c].astype(F32)
        self.ys[c] = self.total[c].astype(BF16)
        for copy in self.second[c]:
            copy.start()

    def end(self, c):
        for copy in self.second[c]:
            copy.wait()
        total = self.total[c]
        for k in range(3):
            total = total + self.yr[c, k].astype(F32)
        return total


class TokenSum:
    def __init__(self, place, mine, got, spread, full, send, recv):
        self.place = place
        self.mine, self.got, self.spread, self.full = mine, got, spread, full
        own = place.chunk(0, 0, 0)
        self.own = own
        self.group = place.z // 4
        groups = place.depth // 4
        self.first, self.third = [], []
        for a, b, step, slot in near_partners():
            device = place.near(a, b, step)
            self.first.append(
                (
                    slot,
                    remote(
                        mine.at[place.chunk(a, b, step)],
                        got.at[slot],
                        send.at[slot],
                        recv.at[slot],
                        device,
                    ),
                )
            )
            self.third.append(
                remote(
                    full.at[own], full.at[own], send.at[24 + slot], recv.at[24 + slot], device
                )
            )
        self.second = [
            remote(
                spread.at[self.group],
                spread.at[self.group],
                send.at[16 + k],
                recv.at[16 + k],
                place.along(4 * k),
            )
            for k in FAR
        ]
        self.groups = groups

    def start(self):
        for _, copy in self.first:
            copy.start()

    def middle(self):
        total = self.mine[self.own].astype(F32)
        for slot, copy in self.first:
            copy.wait_recv()
            total = total + self.got[slot].astype(F32)
        self.spread[self.group] = total.astype(BF16)
        for copy in self.second:
            copy.start()

    def late(self):
        for copy in self.second:
            copy.wait_recv()
        total = self.spread[0].astype(F32)
        for k in range(1, 8):
            total = total + self.spread[k].astype(F32)
        self.full[self.own] = total.astype(BF16)
        for copy in self.third:
            copy.start()

    def end(self):
        for copy in self.third:
            copy.wait_recv()

    def drain(self):
        for _, copy in self.first:
            copy.wait_send()
        for copy in self.second:
            copy.wait_send()
        for copy in self.third:
            copy.wait_send()


NN = (((1,), (0,)), ((), ()))
NT = (((1,), (1,)), ((), ()))
TN = (((0,), (0,)), ((), ()))


def mul(a, b, dims=NN):
    return lax.dot_general(a, b, dims, preferred_element_type=F32)


def greet(place):
    barrier = pltpu.get_barrier_semaphore()
    partners = []
    for step in (2, -2, 1, -1, 0):
        for a in (1, 0):
            for b in (1, 0):
                if a or b or step:
                    partners.append(place.near(a, b, step))
    partners.append({"tensor_0": lax.rem(place.half + 1, 2)})
    for k in (2, 1, 3):
        partners.append({"tensor_1": lax.rem(place.y + k, 4)})
    for device in partners:
        pl.semaphore_signal(barrier, inc=1, device_id=device, device_id_type=MESH_ID)
    return barrier, len(partners)


def tell(place, sem, step):
    for device in (place.along(step), place.along(-step)):
        pl.semaphore_signal(sem, inc=1, device_id=device, device_id_type=MESH_ID)


def kernel(
    normed_hbm,
    query_hbm,
    key_hbm,
    value_hbm,
    down_hbm,
    up_hbm,
    pair_hbm,
    grad_hbm,
    outs,
    down_out,
    up_out,
    pair_out,
    normed,
    qs,
    dos,
    base,
    down_ref,
    up_ref,
    pair_ref,
    kv,
    dkv,
    bias,
    rank_acc,
    up_acc,
    low_s,
    low_r,
    base_r,
    back_s,
    back_r,
    load_sem,
    move_send,
    move_recv,
    reach,
    a_xs,
    a_xr,
    a_ys,
    a_yr,
    a_send,
    a_recv,
    d_xs,
    d_xr,
    d_ys,
    d_yr,
    d_send,
    d_recv,
    e_mine,
    e_got,
    e_spread,
    e_full,
    esend,
    erecv,
    g_mine,
    g_got,
    g_spread,
    g_full,
    gsend,
    grecv,
    h_mine,
    h_got,
    h_spread,
    h_full,
    hsend,
    hrecv,
):
    place = Place()
    tokens, width = normed.shape
    half = tokens // 2
    depth = up_ref.shape[0]
    heads = up_ref.shape[1] // HEAD_SIZE
    tail = low_r.shape[2]
    pad = tail - half

    index = 0

    def fetch(source, target):
        nonlocal index
        copy = pltpu.make_async_copy(source, target, load_sem.at[index])
        copy.start()
        index += 1
        return copy

    down_load = fetch(down_hbm, down_ref)
    halves = [pl.ds(k * (width // 2), width // 2) for k in range(2)]
    normed_loads = [fetch(normed_hbm.at[:, k], normed.at[:, k]) for k in halves]
    barrier, partners = greet(place)
    base_loads = [fetch(key_hbm, base.at[0]), fetch(value_hbm, base.at[1])]
    weight_loads = [fetch(pair_hbm, pair_ref), fetch(up_hbm, up_ref)]

    early = TokenSum(place, e_mine, e_got, e_spread, e_full, esend, erecv)
    late = TokenSum(place, g_mine, g_got, g_spread, g_full, gsend, grecv)
    last = TokenSum(place, h_mine, h_got, h_spread, h_full, hsend, hrecv)
    ranks = TensorSum(place, a_xs, a_xr, a_ys, a_yr, a_send, a_recv)
    rank_grads = TensorSum(place, d_xs, d_xr, d_ys, d_yr, d_send, d_recv)
    base_out = remote(
        base.at[:, pl.ds(half, half), :], base_r, move_send.at[0], move_recv.at[0], place.along(1)
    )
    low_out = [
        remote(
            low_s.at[i, :, pl.ds(tokens - tail, tail)],
            low_r.at[i],
            move_send.at[1 + i],
            move_recv.at[1 + i],
            place.along(1),
        )
        for i in range(2)
    ]
    back = remote(back_s, back_r, move_send.at[3], move_recv.at[3], place.along(-1))

    down_load.wait()
    low = None
    for k, copy in enumerate(normed_loads):
        copy.wait()
        columns = slice(k * (width // 2), (k + 1) * (width // 2))
        term = mul(down_ref[:, columns], normed[:, columns], NT)
        low = term if low is None else low + term
    pl.semaphore_wait(barrier, partners)
    for c in (1, 2, 0):
        ranks.start(c, low[depth * c : depth * (c + 1)])
    for copy in base_loads:
        copy.wait()
    base_out.start()
    tell(place, reach.at[0], 2)
    loads = []
    for source, target in ((query_hbm, qs), (grad_hbm, dos)):
        for h in range(heads):
            for p in range(2):
                loads.append(
                    fetch(
                        source.at[pl.ds(p * half, half), pl.ds(h * HEAD_SIZE, HEAD_SIZE)],
                        target.at[p, pl.ds(h * half, half), :],
                    )
                )

    key_ids = lax.broadcasted_iota(jnp.int32, (half, tokens), 0)
    lanes = lax.broadcasted_iota(jnp.int32, (half, tokens), 1)
    row_ids = jnp.where(lanes < half, lanes, lanes - half)
    bias[...] = jnp.where(key_ids <= row_ids, 0.0, -jnp.inf)
    dkv[...] = jnp.zeros_like(dkv)
    rank_acc[...] = jnp.zeros_like(rank_acc)
    up_acc[...] = jnp.zeros_like(up_acc)

    for c in (1, 2, 0):
        ranks.middle(c)
    pl.semaphore_wait(reach.at[0], 2)
    tell(place, reach.at[1], 4)
    for copy in weight_loads:
        copy.wait()
    for i in range(2):
        low_s[i] = ranks.end(1 + i).astype(BF16)
        low_out[i].start()
        kv[i, half:, :] = (
            base[i].astype(F32) + adapter_scale * mul(low_s[i], pair_ref[i], TN)
        ).astype(BF16)
    low_q = ranks.end(0).astype(BF16)
    low_q32 = low_q.astype(F32)
    query_low = low_q32.T.astype(BF16)
    for copy in loads:
        copy.wait()
    for h in range(heads):
        step = adapter_scale * mul(query_low, up_ref[:, h * HEAD_SIZE : (h + 1) * HEAD_SIZE])
        for p in range(2):
            rows = slice(h * half, (h + 1) * half)
            qs[p, rows, :] = (
                qs[p, rows, :].astype(F32) + step[p * half : (p + 1) * half]
            ).astype(BF16)

    turned = pltpu.roll(low_q32, half, 1)
    in_first = lax.broadcasted_iota(jnp.int32, low_q.shape, 1) < half
    zero = jnp.zeros_like(low_q32)
    wide_low = (
        jnp.concatenate(
            [jnp.where(in_first, low_q32, zero), jnp.where(in_first, zero, turned)], axis=0
        ).astype(BF16),
        jnp.concatenate(
            [jnp.where(in_first, turned, zero), jnp.where(in_first, zero, low_q32)], axis=0
        ).astype(BF16),
    )

    def products(first, count, p, pair):
        rows = slice(pair * tokens, (pair + 1) * tokens)
        keys = kv[0, first : first + count, :]
        values = kv[1, first : first + count, :]
        return mul(keys, qs[p, rows, :], NT), mul(values, dos[p, rows, :], NT)

    def finish(first, count, p, pair, scores, prob_grad):
        scores = scores * (SCALE * LOG2E)
        if count > half:
            scores = jnp.concatenate([scores[:half], scores[half:] + bias[...]], axis=0)
        else:
            scores = scores + bias[...]
        highest = jnp.max(scores, axis=0, keepdims=True)
        weights = jnp.exp2(scores - highest)
        probs = weights * (1.0 / jnp.sum(weights, axis=0, keepdims=True))
        probs_low = probs.astype(BF16)
        row_dot = jnp.sum(probs * prob_grad, axis=0, keepdims=True)
        score_grad = (probs * (prob_grad - row_dot) * SCALE).astype(BF16)
        return probs_low, score_grad

    def spread(first, count, p, pair, probs_low, score_grad):
        rows = slice(pair * tokens, (pair + 1) * tokens)
        keys = kv[0, first : first + count, :]
        values = kv[1, first : first + count, :]
        result = mul(values, probs_low, TN).T.astype(BF16)
        for e in range(2):
            h = 2 * pair + e
            outs[p * half : (p + 1) * half, h * HEAD_SIZE : (h + 1) * HEAD_SIZE] = result[
                e * half : (e + 1) * half
            ]
        query_grad = mul(keys, score_grad, TN).astype(BF16)
        dkv[0, pad + first : pad + first + count, :] += mul(score_grad, qs[p, rows, :])
        dkv[1, pad + first : pad + first + count, :] += mul(probs_low, dos[p, rows, :])
        one, two = 2 * pair, 2 * pair + 1
        ups = jnp.concatenate(
            [up_ref[:, h * HEAD_SIZE : (h + 1) * HEAD_SIZE] for h in (one, two)], axis=0
        )
        rank_acc[p] += mul(ups, query_grad)
        up_acc[pair] += mul(wide_low[p], query_grad, NT)

    def units(*which):
        ready, done = [products(*which[0])], []
        for k, one in enumerate(which):
            if k + 1 < len(which):
                ready.append(products(*which[k + 1]))
            done.append(finish(*one, *ready[k]))
            if k:
                spread(*which[k - 1], *done[k - 1])
        spread(*which[-1], *done[-1])

    pl.semaphore_wait(reach.at[1], 2)
    tell(place, reach.at[2], 8)
    units((half, tokens, 1, 0), (half, tokens, 1, 1))
    base_out.wait()
    for i in range(2):
        low_out[i].wait()
        step = adapter_scale * mul(low_r[i], pair_ref[i], TN)
        kv[i, :half, :] = (base_r[i].astype(F32) + step[pad:]).astype(BF16)
    units((0, tokens, 0, 2), (0, tokens, 0, 3))
    far_grads = [dkv[i, :tail, :].astype(BF16) for i in range(2)]
    for i in range(2):
        back_s[i] = mul(pair_ref[i], far_grads[i], NT).astype(BF16)
    back.start()
    units((half, half, 0, 0), (half, half, 0, 1), (tokens, half, 1, 2), (tokens, half, 1, 3))

    first, second = rank_acc[0], rank_acc[1]
    ours = first[:depth] + pltpu.roll(first[depth:], half, 1)
    theirs = pltpu.roll(second[:depth], half, 1) + second[depth:]
    rank_grads.start(0, jnp.where(in_first, ours, theirs))
    grads = [dkv[i, tail:, :].astype(BF16) for i in range(2)]
    parts = [mul(pair_ref[i], grads[i], NT) for i in range(2)]
    back.wait()
    for i in range(2):
        near = parts[i][:, : tokens - tail]
        far = parts[i][:, tokens - tail :] + back_r[i].astype(F32)
        rank_grads.start(1 + i, jnp.concatenate([near, far], axis=1))
    pair_grads = [
        adapter_scale * (mul(low_s[i], grads[i]) + mul(low_r[i], far_grads[i])) for i in range(2)
    ]
    zeros = jnp.zeros((8, 128), F32)
    for c in range(16):
        h, q = c // 2, c % 2
        top = 16 * (h % 2) + 8 * q
        upper = adapter_scale * up_acc[h // 2, top : top + 8, :]
        lower = pair_grads[c // 2][8 * q : 8 * q + 8] if c < 4 else zeros
        e_mine[c] = jnp.concatenate([upper, lower], axis=0).astype(BF16)
    for c in range(3):
        rank_grads.middle(c)
    early.start()
    rank_grad = jnp.concatenate(
        [(adapter_scale * rank_grads.end(c)).astype(BF16) for c in range(2)], axis=0
    )
    for j in range(8):
        piece = mul(rank_grad, normed[:, 128 * j : 128 * j + 128]).astype(BF16)
        g_mine[2 * j] = piece[:16]
        g_mine[2 * j + 1] = piece[16:]
    late.start()
    pl.semaphore_wait(reach.at[2], 2)
    early.middle()
    rank_grad = (adapter_scale * rank_grads.end(2)).astype(BF16)
    for j in range(8):
        piece = mul(rank_grad, normed[:, 128 * j : 128 * j + 128])
        h_mine[2 * j] = piece[:8].astype(BF16)
        h_mine[2 * j + 1] = piece[8:].astype(BF16)
    last.start()
    late.middle()
    last.middle()
    early.late()
    late.late()
    last.late()
    early.end()
    for c in range(16):
        value = e_full[c].astype(F32)
        up_out[8 * (c % 2) : 8 * (c % 2) + 8, 128 * (c // 2) : 128 * (c // 2) + 128] = value[:8]
        if c < 4:
            pair_out[8 * c : 8 * c + 8, :] = value[8:]
    late.end()
    for c in range(16):
        columns = slice(128 * (c // 2), 128 * (c // 2) + 128)
        down_out[16 * (c % 2) : 16 * (c % 2) + 16, columns] = g_full[c].astype(F32)
    last.end()
    for c in range(16):
        columns = slice(128 * (c // 2), 128 * (c // 2) + 128)
        top = 32 + 8 * (c % 2)
        down_out[top : top + 8, columns] = h_full[c].astype(F32)
    early.drain()
    late.drain()
    last.drain()


def store_kernel(outs, down, up, pair, attended_hbm, down_hbm, up_hbm, pair_hbm, sem):
    rows = attended_hbm.shape[0] // STORES
    copies = []
    for k in range(STORES):
        part = pl.ds(k * rows, rows)
        copies.append(
            pltpu.make_async_copy(outs.at[part], attended_hbm.at[part], sem.at[3 + k])
        )
    for k, (source, target) in enumerate(((down, down_hbm), (up, up_hbm), (pair, pair_hbm))):
        copies.append(pltpu.make_async_copy(source, target, sem.at[k]))
    for copy in copies:
        copy.start()
    for copy in copies:
        copy.wait()


def token_sum_scratch(rows):
    return [
        pltpu.VMEM((16, rows, 128), BF16),
        pltpu.VMEM((16, rows, 128), BF16),
        pltpu.VMEM((8, rows, 128), BF16),
        pltpu.VMEM((16, rows, 128), BF16),
        pltpu.SemaphoreType.DMA((40,)),
        pltpu.SemaphoreType.DMA((40,)),
    ]


def tensor_sum_scratch(chunks, rows, tokens):
    return [
        pltpu.VMEM((chunks, rows, tokens), BF16),
        pltpu.VMEM((chunks, rows, tokens), BF16),
        pltpu.VMEM((chunks, rows, tokens), BF16),
        pltpu.VMEM((chunks, 3, rows, tokens), BF16),
        pltpu.SemaphoreType.DMA((4 * chunks,)),
        pltpu.SemaphoreType.DMA((4 * chunks,)),
    ]


def on_device(normed, query_base, key_base, value_base, down, up, pair, grad):
    vmem = pl.BlockSpec(memory_space=pltpu.VMEM)
    hbm = pl.BlockSpec(memory_space=pltpu.HBM)
    tokens, width = normed.shape[1:]
    depth = up.shape[0]
    ranks = down.shape[1]
    heads = width // HEAD_SIZE
    half = tokens // 2
    tail = 256
    stacked = (2, heads * half, HEAD_SIZE)
    results = pl.pallas_call(
        kernel,
        out_shape=(
            pltpu.VMEM((tokens, width), BF16),
            pltpu.VMEM((ranks, width), F32),
            pltpu.VMEM((depth, width), F32),
            pltpu.VMEM((2 * depth, HEAD_SIZE), F32),
        ),
        in_specs=[hbm] * 8,
        out_specs=(vmem,) * 4,
        scratch_shapes=[
            pltpu.VMEM((tokens, width), BF16),
            pltpu.VMEM(stacked, BF16),
            pltpu.VMEM(stacked, BF16),
            pltpu.VMEM((2, tokens, HEAD_SIZE), BF16),
            pltpu.VMEM((ranks, width), BF16),
            pltpu.VMEM((depth, width), BF16),
            pltpu.VMEM((2, depth, HEAD_SIZE), BF16),
            pltpu.VMEM((2, tokens + half, HEAD_SIZE), BF16),
            pltpu.VMEM((2, tokens + tail, HEAD_SIZE), F32),
            pltpu.VMEM((half, tokens), F32),
            pltpu.VMEM((2, 2 * depth, tokens), F32),
            pltpu.VMEM((heads // 2, 2 * depth, HEAD_SIZE), F32),
            pltpu.VMEM((2, depth, tokens), BF16),
            pltpu.VMEM((2, depth, tail), BF16),
            pltpu.VMEM((2, half, HEAD_SIZE), BF16),
            pltpu.VMEM((2, depth, tail), BF16),
            pltpu.VMEM((2, depth, tail), BF16),
            pltpu.SemaphoreType.DMA((7 + 4 * heads,)),
            pltpu.SemaphoreType.DMA((4,)),
            pltpu.SemaphoreType.DMA((4,)),
            pltpu.SemaphoreType.REGULAR((3,)),
        ]
        + tensor_sum_scratch(3, depth, tokens)
        + tensor_sum_scratch(3, depth, tokens)
        + token_sum_scratch(16)
        + token_sum_scratch(16)
        + token_sum_scratch(8),
        compiler_params=pltpu.CompilerParams(
            collective_id=0, has_side_effects=True, vmem_limit_bytes=60 * 1024 * 1024
        ),
    )(normed[0], query_base[0], key_base[0], value_base[0], down.T, up, pair, grad[0])
    attended, down_grad, up_grad, pair_grad = pl.pallas_call(
        store_kernel,
        out_shape=(
            jax.ShapeDtypeStruct((tokens, width), BF16),
            jax.ShapeDtypeStruct((ranks, width), F32),
            jax.ShapeDtypeStruct((depth, width), F32),
            jax.ShapeDtypeStruct((2 * depth, HEAD_SIZE), F32),
        ),
        in_specs=[vmem] * 4,
        out_specs=(hbm,) * 4,
        scratch_shapes=[pltpu.SemaphoreType.DMA((3 + STORES,))],
        compiler_params=pltpu.CompilerParams(vmem_limit_bytes=1024 * 1024),
    )(*results)
    return (attended[None], down_grad.T, up_grad, pair_grad.reshape(2, depth, -1))


def solution(mesh):
    split = Mesh(
        mesh.devices.reshape(2, 2, mesh.shape["context"], 2, 4),
        ("dp_0", "dp_1", "context", "tensor_0", "tensor_1"),
    )
    placed = (
        P(DP, "context", TENSOR),
        P(DP, "context", TENSOR),
        P(DP, "context", TENSOR),
        P(DP, "context", TENSOR),
        P(TENSOR, None),
        P(None, TENSOR),
        P(None, None, TENSOR),
        P(DP, "context", TENSOR),
    )
    return jax.shard_map(
        on_device,
        mesh=split,
        in_specs=placed,
        out_specs=(
            P(DP, "context", TENSOR),
            P(TENSOR, None),
            P(None, TENSOR),
            P(None, None, TENSOR),
        ),
        check_vma=False,
    )
```

```python
import jax
import jax.numpy as jnp
from jax import lax
from jax.experimental import pallas as pl
from jax.experimental.pallas import tpu as pltpu
from jax.sharding import Mesh
from jax.sharding import PartitionSpec as P

HEAD_SIZE = 128
TENSOR = ("tensor_0", "tensor_1")
DP = ("dp_0", "dp_1")
SCALE = HEAD_SIZE**-0.5
LOG2E = 1.4426950408889634
adapter_scale = 2.0

MESH_ID = pl.DeviceIdType.MESH
F32 = jnp.float32
BF16 = jnp.bfloat16
STEPS = (2, 1, -1, 0)
FAR = (4, 3, 5, 2, 6, 1, 7)
STORES = 4


class Place:
    def __init__(self):
        self.x = lax.axis_index("dp_0")
        self.core = lax.axis_index("dp_1")
        self.z = lax.axis_index("context")
        self.half = lax.axis_index("tensor_0")
        self.y = lax.axis_index("tensor_1")
        self.depth = lax.axis_size("context")

    def near(self, a, b, step):
        z = lax.rem(self.z + step + self.depth, self.depth)
        return {
            "dp_0": lax.rem(self.x + a, 2),
            "dp_1": lax.rem(self.core + b, 2),
            "context": z,
        }

    def along(self, step):
        return {"context": lax.rem(self.z + step + self.depth, self.depth)}

    def chunk(self, a, b, step):
        x = lax.rem(self.x + a, 2)
        core = lax.rem(self.core + b, 2)
        return (x * 2 + core) * 4 + lax.rem(self.z + step + 4, 4)


def near_partners():
    for step in STEPS:
        for a in (1, 0):
            for b in (1, 0):
                if a or b or step:
                    yield a, b, step, (a * 2 + b) * 4 + STEPS.index(step)


def remote(src, dst, send_sem, recv_sem, device):
    return pltpu.make_async_remote_copy(
        src_ref=src,
        dst_ref=dst,
        send_sem=send_sem,
        recv_sem=recv_sem,
        device_id=device,
        device_id_type=MESH_ID,
    )


class TensorSum:
    def __init__(self, place, xs, xr, ys, yr, send, recv):
        self.xs, self.xr, self.ys, self.yr = xs, xr, ys, yr
        half = lax.rem(place.half + 1, 2)
        chunks = range(xs.shape[0])
        self.first = [
            remote(
                xs.at[c], xr.at[c], send.at[4 * c], recv.at[4 * c], {"tensor_0": half}
            )
            for c in chunks
        ]
        self.second = [
            [
                remote(
                    ys.at[c],
                    yr.at[c, k - 1],
                    send.at[4 * c + k],
                    recv.at[4 * c + k],
                    {"tensor_1": lax.rem(place.y + k, 4)},
                )
                for k in (2, 1, 3)
            ]
            for c in chunks
        ]
        self.part, self.total = {}, {}

    def start(self, c, part):
        self.part[c] = part
        self.xs[c] = part.astype(BF16)
        self.first[c].start()

    def middle(self, c):
        self.first[c].wait()
        self.total[c] = self.part[c] + self.xr[c].astype(F32)
        self.ys[c] = self.total[c].astype(BF16)
        for copy in self.second[c]:
            copy.start()

    def end(self, c):
        for copy in self.second[c]:
            copy.wait()
        total = self.total[c]
        for k in range(3):
            total = total + self.yr[c, k].astype(F32)
        return total


class TokenSum:
    def __init__(self, place, mine, got, spread, full, send, recv):
        self.place = place
        self.mine, self.got, self.spread, self.full = mine, got, spread, full
        own = place.chunk(0, 0, 0)
        self.own = own
        self.group = place.z // 4
        groups = place.depth // 4
        self.first, self.third = [], []
        for a, b, step, slot in near_partners():
            device = place.near(a, b, step)
            self.first.append(
                (
                    slot,
                    remote(
                        mine.at[place.chunk(a, b, step)],
                        got.at[slot],
                        send.at[slot],
                        recv.at[slot],
                        device,
                    ),
                )
            )
            self.third.append(
                remote(
                    full.at[own], full.at[own], send.at[24 + slot], recv.at[24 + slot], device
                )
            )
        self.second = [
            remote(
                spread.at[self.group],
                spread.at[self.group],
                send.at[16 + k],
                recv.at[16 + k],
                place.along(4 * k),
            )
            for k in FAR
        ]
        self.groups = groups

    def start(self):
        for _, copy in self.first:
            copy.start()

    def middle(self):
        total = self.mine[self.own].astype(F32)
        for slot, copy in self.first:
            copy.wait_recv()
            total = total + self.got[slot].astype(F32)
        self.spread[self.group] = total.astype(BF16)
        for copy in self.second:
            copy.start()

    def late(self):
        for copy in self.second:
            copy.wait_recv()
        total = self.spread[0].astype(F32)
        for k in range(1, 8):
            total = total + self.spread[k].astype(F32)
        self.full[self.own] = total.astype(BF16)
        for copy in self.third:
            copy.start()

    def end(self):
        for copy in self.third:
            copy.wait_recv()

    def drain(self):
        for _, copy in self.first:
            copy.wait_send()
        for copy in self.second:
            copy.wait_send()
        for copy in self.third:
            copy.wait_send()


NN = (((1,), (0,)), ((), ()))
NT = (((1,), (1,)), ((), ()))
TN = (((0,), (0,)), ((), ()))


def mul(a, b, dims=NN):
    return lax.dot_general(a, b, dims, preferred_element_type=F32)


def greet(place):
    barrier = pltpu.get_barrier_semaphore()
    partners = []
    for step in (2, -2, 1, -1, 0):
        for a in (1, 0):
            for b in (1, 0):
                if a or b or step:
                    partners.append(place.near(a, b, step))
    partners.append({"tensor_0": lax.rem(place.half + 1, 2)})
    for k in (2, 1, 3):
        partners.append({"tensor_1": lax.rem(place.y + k, 4)})
    for device in partners:
        pl.semaphore_signal(barrier, inc=1, device_id=device, device_id_type=MESH_ID)
    return barrier, len(partners)


def tell(place, sem, step):
    for device in (place.along(step), place.along(-step)):
        pl.semaphore_signal(sem, inc=1, device_id=device, device_id_type=MESH_ID)


def kernel(
    normed_hbm,
    query_hbm,
    key_hbm,
    value_hbm,
    down_hbm,
    up_hbm,
    pair_hbm,
    grad_hbm,
    outs,
    down_out,
    up_out,
    pair_out,
    normed,
    qs,
    dos,
    base,
    down_ref,
    up_ref,
    pair_ref,
    kv,
    dkv,
    bias,
    rank_acc,
    up_acc,
    low_s,
    low_r,
    base_r,
    back_s,
    back_r,
    load_sem,
    move_send,
    move_recv,
    reach,
    a_xs,
    a_xr,
    a_ys,
    a_yr,
    a_send,
    a_recv,
    d_xs,
    d_xr,
    d_ys,
    d_yr,
    d_send,
    d_recv,
    e_mine,
    e_got,
    e_spread,
    e_full,
    esend,
    erecv,
    g_mine,
    g_got,
    g_spread,
    g_full,
    gsend,
    grecv,
):
    place = Place()
    tokens, width = normed.shape
    half = tokens // 2
    depth = up_ref.shape[0]
    heads = up_ref.shape[1] // HEAD_SIZE
    tail = low_r.shape[2]
    pad = tail - half

    index = 0

    def fetch(source, target):
        nonlocal index
        copy = pltpu.make_async_copy(source, target, load_sem.at[index])
        copy.start()
        index += 1
        return copy

    down_load = fetch(down_hbm, down_ref)
    halves = [pl.ds(k * (width // 2), width // 2) for k in range(2)]
    normed_loads = [fetch(normed_hbm.at[:, k], normed.at[:, k]) for k in halves]
    barrier, partners = greet(place)
    base_loads = [fetch(key_hbm, base.at[0]), fetch(value_hbm, base.at[1])]
    weight_loads = [fetch(pair_hbm, pair_ref), fetch(up_hbm, up_ref)]

    early = TokenSum(place, e_mine, e_got, e_spread, e_full, esend, erecv)
    late = TokenSum(place, g_mine, g_got, g_spread, g_full, gsend, grecv)
    ranks = TensorSum(place, a_xs, a_xr, a_ys, a_yr, a_send, a_recv)
    rank_grads = TensorSum(place, d_xs, d_xr, d_ys, d_yr, d_send, d_recv)
    base_out = remote(
        base.at[:, pl.ds(half, half), :], base_r, move_send.at[0], move_recv.at[0], place.along(1)
    )
    low_out = [
        remote(
            low_s.at[i, :, pl.ds(tokens - tail, tail)],
            low_r.at[i],
            move_send.at[1 + i],
            move_recv.at[1 + i],
            place.along(1),
        )
        for i in range(2)
    ]
    back = remote(back_s, back_r, move_send.at[3], move_recv.at[3], place.along(-1))

    down_load.wait()
    low = None
    for k, copy in enumerate(normed_loads):
        copy.wait()
        columns = slice(k * (width // 2), (k + 1) * (width // 2))
        term = mul(down_ref[:, columns], normed[:, columns], NT)
        low = term if low is None else low + term
    pl.semaphore_wait(barrier, partners)
    for c in (1, 2, 0):
        ranks.start(c, low[depth * c : depth * (c + 1)])
    for copy in base_loads:
        copy.wait()
    base_out.start()
    tell(place, reach.at[0], 2)
    loads = []
    for source, target in ((query_hbm, qs), (grad_hbm, dos)):
        for h in range(heads):
            for p in range(2):
                loads.append(
                    fetch(
                        source.at[pl.ds(p * half, half), pl.ds(h * HEAD_SIZE, HEAD_SIZE)],
                        target.at[p, pl.ds(h * half, half), :],
                    )
                )

    key_ids = lax.broadcasted_iota(jnp.int32, (half, tokens), 0)
    lanes = lax.broadcasted_iota(jnp.int32, (half, tokens), 1)
    row_ids = jnp.where(lanes < half, lanes, lanes - half)
    bias[...] = jnp.where(key_ids <= row_ids, 0.0, -jnp.inf)
    dkv[...] = jnp.zeros_like(dkv)
    rank_acc[...] = jnp.zeros_like(rank_acc)
    up_acc[...] = jnp.zeros_like(up_acc)

    for c in (1, 2, 0):
        ranks.middle(c)
    pl.semaphore_wait(reach.at[0], 2)
    tell(place, reach.at[1], 4)
    for copy in weight_loads:
        copy.wait()
    for i in range(2):
        low_s[i] = ranks.end(1 + i).astype(BF16)
        low_out[i].start()
        kv[i, half:, :] = (
            base[i].astype(F32) + adapter_scale * mul(low_s[i], pair_ref[i], TN)
        ).astype(BF16)
    low_q = ranks.end(0).astype(BF16)
    low_q32 = low_q.astype(F32)
    query_low = low_q32.T.astype(BF16)
    for copy in loads:
        copy.wait()
    for h in range(heads):
        step = adapter_scale * mul(query_low, up_ref[:, h * HEAD_SIZE : (h + 1) * HEAD_SIZE])
        for p in range(2):
            rows = slice(h * half, (h + 1) * half)
            qs[p, rows, :] = (
                qs[p, rows, :].astype(F32) + step[p * half : (p + 1) * half]
            ).astype(BF16)

    turned = pltpu.roll(low_q32, half, 1)
    in_first = lax.broadcasted_iota(jnp.int32, low_q.shape, 1) < half
    zero = jnp.zeros_like(low_q32)
    wide_low = (
        jnp.concatenate(
            [jnp.where(in_first, low_q32, zero), jnp.where(in_first, zero, turned)], axis=0
        ).astype(BF16),
        jnp.concatenate(
            [jnp.where(in_first, turned, zero), jnp.where(in_first, zero, low_q32)], axis=0
        ).astype(BF16),
    )

    def products(first, count, p, pair):
        rows = slice(pair * tokens, (pair + 1) * tokens)
        keys = kv[0, first : first + count, :]
        values = kv[1, first : first + count, :]
        return mul(keys, qs[p, rows, :], NT), mul(values, dos[p, rows, :], NT)

    def finish(first, count, p, pair, scores, prob_grad):
        scores = scores * (SCALE * LOG2E)
        if count > half:
            scores = jnp.concatenate([scores[:half], scores[half:] + bias[...]], axis=0)
        else:
            scores = scores + bias[...]
        highest = jnp.max(scores, axis=0, keepdims=True)
        weights = jnp.exp2(scores - highest)
        probs = weights * (1.0 / jnp.sum(weights, axis=0, keepdims=True))
        probs_low = probs.astype(BF16)
        row_dot = jnp.sum(probs * prob_grad, axis=0, keepdims=True)
        score_grad = (probs * (prob_grad - row_dot) * SCALE).astype(BF16)
        return probs_low, score_grad

    def spread(first, count, p, pair, probs_low, score_grad):
        rows = slice(pair * tokens, (pair + 1) * tokens)
        keys = kv[0, first : first + count, :]
        values = kv[1, first : first + count, :]
        result = mul(values, probs_low, TN).T.astype(BF16)
        for e in range(2):
            h = 2 * pair + e
            outs[p * half : (p + 1) * half, h * HEAD_SIZE : (h + 1) * HEAD_SIZE] = result[
                e * half : (e + 1) * half
            ]
        query_grad = mul(keys, score_grad, TN).astype(BF16)
        dkv[0, pad + first : pad + first + count, :] += mul(score_grad, qs[p, rows, :])
        dkv[1, pad + first : pad + first + count, :] += mul(probs_low, dos[p, rows, :])
        one, two = 2 * pair, 2 * pair + 1
        ups = jnp.concatenate(
            [up_ref[:, h * HEAD_SIZE : (h + 1) * HEAD_SIZE] for h in (one, two)], axis=0
        )
        rank_acc[p] += mul(ups, query_grad)
        up_acc[pair] += mul(wide_low[p], query_grad, NT)

    def units(*which):
        ready, done = [products(*which[0])], []
        for k, one in enumerate(which):
            if k + 1 < len(which):
                ready.append(products(*which[k + 1]))
            done.append(finish(*one, *ready[k]))
            if k:
                spread(*which[k - 1], *done[k - 1])
        spread(*which[-1], *done[-1])

    pl.semaphore_wait(reach.at[1], 2)
    tell(place, reach.at[2], 8)
    units((half, tokens, 1, 0), (half, tokens, 1, 1))
    base_out.wait()
    for i in range(2):
        low_out[i].wait()
        step = adapter_scale * mul(low_r[i], pair_ref[i], TN)
        kv[i, :half, :] = (base_r[i].astype(F32) + step[pad:]).astype(BF16)
    units((0, tokens, 0, 2), (0, tokens, 0, 3))
    far_grads = [dkv[i, :tail, :].astype(BF16) for i in range(2)]
    for i in range(2):
        back_s[i] = mul(pair_ref[i], far_grads[i], NT).astype(BF16)
    back.start()
    units((half, half, 0, 0), (half, half, 0, 1), (tokens, half, 1, 2), (tokens, half, 1, 3))

    first, second = rank_acc[0], rank_acc[1]
    ours = first[:depth] + pltpu.roll(first[depth:], half, 1)
    theirs = pltpu.roll(second[:depth], half, 1) + second[depth:]
    rank_grads.start(0, jnp.where(in_first, ours, theirs))
    grads = [dkv[i, tail:, :].astype(BF16) for i in range(2)]
    parts = [mul(pair_ref[i], grads[i], NT) for i in range(2)]
    back.wait()
    for i in range(2):
        near = parts[i][:, : tokens - tail]
        far = parts[i][:, tokens - tail :] + back_r[i].astype(F32)
        rank_grads.start(1 + i, jnp.concatenate([near, far], axis=1))
    pair_grads = [
        adapter_scale * (mul(low_s[i], grads[i]) + mul(low_r[i], far_grads[i])) for i in range(2)
    ]
    zeros = jnp.zeros((8, 128), F32)
    for c in range(16):
        h, q = c // 2, c % 2
        top = 16 * (h % 2) + 8 * q
        upper = adapter_scale * up_acc[h // 2, top : top + 8, :]
        lower = pair_grads[c // 2][8 * q : 8 * q + 8] if c < 4 else zeros
        e_mine[c] = jnp.concatenate([upper, lower], axis=0).astype(BF16)
    for c in range(3):
        rank_grads.middle(c)
    early.start()
    rank_grad = jnp.concatenate(
        [(adapter_scale * rank_grads.end(c)).astype(BF16) for c in range(3)], axis=0
    )
    for j in range(8):
        columns = slice(128 * j, 128 * j + 128)
        down = mul(rank_grad, normed[:, columns])
        g_mine[2 * j] = down[:24].astype(BF16)
        g_mine[2 * j + 1] = down[24:].astype(BF16)
    late.start()
    pl.semaphore_wait(reach.at[2], 2)
    early.middle()
    late.middle()
    early.late()
    late.late()
    early.end()
    for c in range(16):
        value = e_full[c].astype(F32)
        up_out[8 * (c % 2) : 8 * (c % 2) + 8, 128 * (c // 2) : 128 * (c // 2) + 128] = value[:8]
        if c < 4:
            pair_out[8 * c : 8 * c + 8, :] = value[8:]
    late.end()
    for c in range(16):
        down_out[24 * (c % 2) : 24 * (c % 2) + 24, 128 * (c // 2) : 128 * (c // 2) + 128] = g_full[
            c
        ].astype(F32)
    early.drain()
    late.drain()


def store_kernel(outs, down, up, pair, attended_hbm, down_hbm, up_hbm, pair_hbm, sem):
    rows = attended_hbm.shape[0] // STORES
    copies = []
    for k in range(STORES):
        part = pl.ds(k * rows, rows)
        copies.append(
            pltpu.make_async_copy(outs.at[part], attended_hbm.at[part], sem.at[3 + k])
        )
    for k, (source, target) in enumerate(((down, down_hbm), (up, up_hbm), (pair, pair_hbm))):
        copies.append(pltpu.make_async_copy(source, target, sem.at[k]))
    for copy in copies:
        copy.start()
    for copy in copies:
        copy.wait()


def token_sum_scratch(rows):
    return [
        pltpu.VMEM((16, rows, 128), BF16),
        pltpu.VMEM((16, rows, 128), BF16),
        pltpu.VMEM((8, rows, 128), BF16),
        pltpu.VMEM((16, rows, 128), BF16),
        pltpu.SemaphoreType.DMA((40,)),
        pltpu.SemaphoreType.DMA((40,)),
    ]


def tensor_sum_scratch(chunks, rows, tokens):
    return [
        pltpu.VMEM((chunks, rows, tokens), BF16),
        pltpu.VMEM((chunks, rows, tokens), BF16),
        pltpu.VMEM((chunks, rows, tokens), BF16),
        pltpu.VMEM((chunks, 3, rows, tokens), BF16),
        pltpu.SemaphoreType.DMA((4 * chunks,)),
        pltpu.SemaphoreType.DMA((4 * chunks,)),
    ]


def on_device(normed, query_base, key_base, value_base, down, up, pair, grad):
    vmem = pl.BlockSpec(memory_space=pltpu.VMEM)
    hbm = pl.BlockSpec(memory_space=pltpu.HBM)
    tokens, width = normed.shape[1:]
    depth = up.shape[0]
    ranks = down.shape[1]
    heads = width // HEAD_SIZE
    half = tokens // 2
    tail = 256
    stacked = (2, heads * half, HEAD_SIZE)
    results = pl.pallas_call(
        kernel,
        out_shape=(
            pltpu.VMEM((tokens, width), BF16),
            pltpu.VMEM((ranks, width), F32),
            pltpu.VMEM((depth, width), F32),
            pltpu.VMEM((2 * depth, HEAD_SIZE), F32),
        ),
        in_specs=[hbm] * 8,
        out_specs=(vmem,) * 4,
        scratch_shapes=[
            pltpu.VMEM((tokens, width), BF16),
            pltpu.VMEM(stacked, BF16),
            pltpu.VMEM(stacked, BF16),
            pltpu.VMEM((2, tokens, HEAD_SIZE), BF16),
            pltpu.VMEM((ranks, width), BF16),
            pltpu.VMEM((depth, width), BF16),
            pltpu.VMEM((2, depth, HEAD_SIZE), BF16),
            pltpu.VMEM((2, tokens + half, HEAD_SIZE), BF16),
            pltpu.VMEM((2, tokens + tail, HEAD_SIZE), F32),
            pltpu.VMEM((half, tokens), F32),
            pltpu.VMEM((2, 2 * depth, tokens), F32),
            pltpu.VMEM((heads // 2, 2 * depth, HEAD_SIZE), F32),
            pltpu.VMEM((2, depth, tokens), BF16),
            pltpu.VMEM((2, depth, tail), BF16),
            pltpu.VMEM((2, half, HEAD_SIZE), BF16),
            pltpu.VMEM((2, depth, tail), BF16),
            pltpu.VMEM((2, depth, tail), BF16),
            pltpu.SemaphoreType.DMA((7 + 4 * heads,)),
            pltpu.SemaphoreType.DMA((4,)),
            pltpu.SemaphoreType.DMA((4,)),
            pltpu.SemaphoreType.REGULAR((3,)),
        ]
        + tensor_sum_scratch(3, depth, tokens)
        + tensor_sum_scratch(3, depth, tokens)
        + token_sum_scratch(16)
        + token_sum_scratch(24),
        compiler_params=pltpu.CompilerParams(
            collective_id=0, has_side_effects=True, vmem_limit_bytes=60 * 1024 * 1024
        ),
    )(normed[0], query_base[0], key_base[0], value_base[0], down.T, up, pair, grad[0])
    attended, down_grad, up_grad, pair_grad = pl.pallas_call(
        store_kernel,
        out_shape=(
            jax.ShapeDtypeStruct((tokens, width), BF16),
            jax.ShapeDtypeStruct((ranks, width), F32),
            jax.ShapeDtypeStruct((depth, width), F32),
            jax.ShapeDtypeStruct((2 * depth, HEAD_SIZE), F32),
        ),
        in_specs=[vmem] * 4,
        out_specs=(hbm,) * 4,
        scratch_shapes=[pltpu.SemaphoreType.DMA((3 + STORES,))],
        compiler_params=pltpu.CompilerParams(vmem_limit_bytes=1024 * 1024),
    )(*results)
    return (attended[None], down_grad.T, up_grad, pair_grad.reshape(2, depth, -1))


def solution(mesh):
    split = Mesh(
        mesh.devices.reshape(2, 2, mesh.shape["context"], 2, 4),
        ("dp_0", "dp_1", "context", "tensor_0", "tensor_1"),
    )
    placed = (
        P(DP, "context", TENSOR),
        P(DP, "context", TENSOR),
        P(DP, "context", TENSOR),
        P(DP, "context", TENSOR),
        P(TENSOR, None),
        P(None, TENSOR),
        P(None, None, TENSOR),
        P(DP, "context", TENSOR),
    )
    return jax.shard_map(
        on_device,
        mesh=split,
        in_specs=placed,
        out_specs=(
            P(DP, "context", TENSOR),
            P(TENSOR, None),
            P(None, TENSOR),
            P(None, None, TENSOR),
        ),
        check_vma=False,
    )
```
